128 devices in a mesh: com: 32 (over x, z, y_hi), arc: 4 (over y_lo, core).
Axes of the slice: x: 4, y: 4 (y_hi: 2, y_lo: 2; y = y_hi * 2 + y_lo), z: 4, core: 2. Of those that a mesh axis runs over, the one named last changes fastest.
Arguments:
- lfactor: float32 [64, 768, 768], P('com'), as said below
- links: float32 [64, 768, 4096], P('com', None, 'arc'), may hold values from -0.0546875 to 0.0546875
- usage: int32 [64, 4096], P('com', 'arc'), may hold values 0 or 1
- demands: bfloat16 [64, 768, 256], P('com'), may hold values from -6 to 6
- damping: float32 [4096], P('arc'), may hold values from 0.2 to 1
Outputs:
- schur: float32 [4096, 4096], P('com', 'arc')
- newton_y: float32 [4096, 256], P('arc')
- steps: float32 [64, 768, 256], P('com', None, 'arc')
The draws below stay inside these ranges and needn't reach their ends.
Inputs may be any that keep to these rules, and one draw needn't show every extreme that they name: lfactor[k] is lower triangular with its diagonal between 1 and 2.
All inputs are finite; a program needn't handle non-finite values. No bound on the sum of `usage` on one device may be relied on, other than what follows from the above.
Results may differ from the reference program's by a relative error of at most 0.003.
Values may be sent and summed in bfloat16 or wider, within the bound.
A program may use at most 192 MiB of HBM per device.

```python
import math
import jax
import jax.numpy as jnp
from jax import lax

NODES = 768
ARCS = 4096
SCEN = 256
COMS = 64


def draw_lfactor(key, part):
    key_diag, key_off = jax.random.split(jax.random.fold_in(key, 11))
    diagonal = jnp.exp(jax.random.uniform(key_diag, (COMS, NODES), jnp.float32, 0.0, math.log(2.0)))
    spread = jax.random.normal(key_off, (COMS, NODES, NODES), jnp.float32) * (0.4 / math.sqrt(NODES))
    row_index = jnp.arange(NODES)[:, None]
    col_index = jnp.arange(NODES)[None, :]
    below = (row_index > col_index).astype(jnp.float32)
    on_diag = (row_index == col_index).astype(jnp.float32)
    return spread * below[None] + diagonal[:, :, None] * on_diag[None]


def plant(result, rng, least, high):
    spot = [jax.random.randint(jax.random.fold_in(rng, axis), (), 0, length) for axis, length in enumerate(result.shape)]
    widest = result.shape.index(max(result.shape))
    beside = spot[:widest] + [(spot[widest] + 1) % result.shape[widest]] + spot[widest + 1:]
    return result.at[tuple(spot)].set(least).at[tuple(beside)].set(high)


def spiked(values, stream_key, source, target, shards_of, factor):
    def block_of(dim):
        return (jnp.arange(values.shape[dim]) // (values.shape[dim] // shards_of)).reshape((-1,) + (1,) * (values.ndim - 1 - dim))

    one_side = jax.random.permutation(stream_key, shards_of)[block_of(target)]
    far = (block_of(target) + shards_of // 2) % shards_of
    return jnp.where((block_of(source) == one_side) | (block_of(source) == far), factor * values, values)


def level_of(rng, dims, cuts, low, high):
    def one(position, shards_of):
        draws = jax.random.uniform(jax.random.fold_in(jax.random.fold_in(rng, 6), position), (shards_of,), jnp.float32, low / len(cuts), high / len(cuts))
        return jnp.repeat(jnp.exp(draws), dims[position] // shards_of).reshape((-1,) + (1,) * (len(dims) - position - 1))

    gain = one(*cuts[0])
    for cut in cuts[1:]:
        gain = gain * one(*cut)
    return gain


def noise(stream_key, dims, width, limit, cuts=(), held_as=jnp.bfloat16):
    loudness = level_of(stream_key, dims, cuts, -0.22, 0.18) if cuts else 1.0
    entries = jax.random.normal(stream_key, dims, jnp.float32) * width * loudness
    return jnp.minimum(jnp.maximum(entries, -limit), limit).astype(held_as)


def bell_draw_with(rng, dims, deviation, reach, cuts, heavy, held_as=jnp.bfloat16):
    values = deviation * jax.random.normal(rng, dims, jnp.float32)
    if cuts:
        values = values * level_of(rng, dims, cuts, -0.22, 0.18)
    return jnp.clip(spiked(values, jax.random.fold_in(rng, 3), *heavy), -reach, reach).astype(held_as)


def setup_inputs(seed: int = 0) -> dict:
    key_of = jax.random.split(jax.random.key(seed), 6)
    return {
        "lfactor": draw_lfactor(jax.random.fold_in(key_of[5], 71), 0),
        "links": bell_draw_with(key_of[1], (COMS, NODES, ARCS), (COMS * NODES) ** -0.5, 0.0546875, ((0, 32), (2, 4)), (0, 2, 32, 2.75), jnp.float32),
        "usage": plant((jax.random.randint(key_of[2], (COMS, ARCS), 0, 4) < 3).astype(jnp.int32), jax.random.fold_in(key_of[2], 1), 0, 1),
        "demands": noise(key_of[3], (COMS, NODES, SCEN), 1.0, 6.0, ((0, 32),)),
        "damping": jnp.clip(0.2 + 0.8 * jax.random.uniform(key_of[4], (ARCS,), jnp.float32) ** level_of(key_of[4], (ARCS,), ((0, 4),), -0.2, 0.2), 0.2, 1.0),
    }


def reference(lfactor, links, usage, demands, damping):
    coupling = links * usage[:, None, :].astype(jnp.float32)

    def forward_one(pair):
        factor, coupling_block = pair
        return jax.scipy.linalg.solve_triangular(factor, coupling_block, lower=True).astype(jnp.bfloat16)
    transformed = lax.map(forward_one, (lfactor, coupling))

    def accumulate(carry, items):
        panel_one, demand_one = items
        panel_wide = panel_one.astype(jnp.float32)
        demand_wide = demand_one.astype(jnp.float32)
        schur_sum = carry[0] + jnp.dot(panel_wide.T, panel_wide, precision=lax.Precision.HIGHEST)
        rhs_sum = carry[1] + jnp.dot(panel_wide.T, demand_wide, precision=lax.Precision.HIGHEST)
        return ((schur_sum, rhs_sum), None)
    start_carry = (jnp.zeros((ARCS, ARCS), jnp.float32), jnp.zeros((ARCS, SCEN), jnp.float32))
    (schur, rhs), _ = lax.scan(accumulate, start_carry, (transformed, demands))
    product = jnp.dot(schur, rhs, precision=lax.Precision.HIGHEST)
    newton_y = rhs - damping[:, None] * product
    rounded_y = newton_y.astype(jnp.bfloat16)

    def backward_one(triple):
        factor, panel_one, demand_one = triple
        correction = jnp.dot(panel_one.astype(jnp.float32), rounded_y.astype(jnp.float32), preferred_element_type=jnp.float32)
        return jax.scipy.linalg.solve_triangular(factor, demand_one.astype(jnp.float32) - correction, lower=True, trans=1)
    steps = lax.map(backward_one, (lfactor, transformed, demands))
    return (schur, newton_y, steps)
```

```python
import functools
import jax
import jax.numpy as jnp
from jax import lax
from jax.experimental import pallas as pl
from jax.experimental.pallas import tpu as pltpu
from jax.sharding import PartitionSpec as P

F32, BF16 = jnp.float32, jnp.bfloat16
VM = pl.BlockSpec(memory_space=pltpu.VMEM)
ANY = pl.BlockSpec(memory_space=pl.ANY)


def halves(x):
    high = x.astype(BF16)
    return high, (x - high.astype(F32)).astype(BF16)


def mm(a, b):
    return jnp.dot(a, b, preferred_element_type=F32)


def mm3(a, b):
    return mm(a[0], b[0]) + (mm(a[0], b[1]) + mm(a[1], b[0]))


def front_kernel(lf, links, usage, dem, t_out, tt_out, rhs_out, dh, dl, lh, ll, cbuf, mbuf, xbuf, xinv, sems):
    n, nodes, _ = lf.shape
    tiles = nodes // 128
    rows = n * tiles
    copies = [pltpu.make_async_copy(links.at[k], cbuf.at[k], sems.at[k]) for k in range(n)]
    for c in copies:
        c.start()
    lane = lax.broadcasted_iota(jnp.int32, (32, 128), 1)
    for k in range(n):
        for t in range(tiles):
            acc = jnp.zeros((32, 128), F32)
            for p in range(4):
                part = lf[k, t * 128 + 32 * p:t * 128 + 32 * p + 32, t * 128:t * 128 + 128]
                acc = jnp.where(lane // 32 == p, part, acc)
            mbuf[pl.ds((k * tiles + t) * 32, 32), :] = acc
    seg = lax.broadcasted_iota(jnp.int32, (rows, 128), 1)
    for i in range(32):
        a = mbuf[pl.ds(i, rows, stride=32), :]

        def spread(j):
            out = jnp.broadcast_to(a[:, j:j + 1], (rows, 128))
            for p in range(1, 4):
                out = jnp.where(seg // 32 == p, jnp.broadcast_to(a[:, 32 * p + j:32 * p + j + 1], (rows, 128)), out)
            return out

        acc = jnp.where(seg % 32 == i, 1.0, 0.0).astype(F32)
        for j in range(i):
            acc = acc - spread(j) * xbuf[pl.ds(j, rows, stride=32), :]
        xbuf[pl.ds(i, rows, stride=32), :] = acc / spread(i)
    for k in range(n):
        for t in range(tiles):
            part = xbuf[pl.ds((k * tiles + t) * 32, 32), :]
            for p in range(4):
                at = t * 128 + 32 * p
                here = (t % 2) * 128
                xinv[k, at:at + 32, here:here + 128] = jnp.where(lane // 32 == p, part, 0.0)
                xinv[k, at:at + 32, 128 - here:256 - here] = jnp.zeros((32, 128), F32)

    r = lax.broadcasted_iota(jnp.int32, (256, 256), 0)
    c = lax.broadcasted_iota(jnp.int32, (256, 256), 1)

    @pl.loop(0, nodes // 256)
    def _(b):
        at = pl.multiple_of(b * 256, 256)
        block = [lf[k, pl.ds(at, 256), pl.ds(at, 256)] for k in range(n)]
        inv = [xinv[k, pl.ds(at, 256), :] for k in range(n)]
        for s in (32, 64, 128):
            keep = (r // (2 * s) == c // (2 * s)) & (r // s > c // s)
            for k in range(n):
                x = halves(inv[k])
                y = mm3(x, halves(jnp.where(keep, block[k], 0.0)))
                inv[k] = inv[k] - mm3(halves(y), x)
        for k in range(n):
            dh[k, pl.ds(at, 256), :], dl[k, pl.ds(at, 256), :] = halves(inv[k])

    for k in range(n):
        for b in range(1, nodes // 256):
            for e in range(b):
                s = (k, slice(256 * b, 256 * b + 256), slice(256 * e, 256 * e + 256))
                lh[s], ll[s] = halves(lf[s])
        copies[k].wait()

    width = 512
    arcs = cbuf.shape[2]
    blocks = nodes // 256
    for k in range(n):
        @pl.loop(0, arcs // width)
        def _(q):
            cols = pl.ds(pl.multiple_of(q * width, width), width)
            use = usage[pl.ds(k, 1), cols].astype(F32)
            done = []
            for b in range(blocks):
                rest = cbuf[k, 256 * b:256 * b + 256, cols] * use
                for e in range(b):
                    s = (k, slice(256 * b, 256 * b + 256), slice(256 * e, 256 * e + 256))
                    rest = rest - mm3((lh[s], ll[s]), done[e])
                s = (k, slice(256 * b, 256 * b + 256))
                out = mm3((dh[s], dl[s]), halves(rest))
                done.append(halves(out))
                t_out[k * nodes + 256 * b:k * nodes + 256 * b + 256, cols] = done[b][0]
                tt_out[cols, k * nodes + 256 * b:k * nodes + 256 * b + 256] = out.T.astype(BF16)

    @pl.loop(0, arcs // 256)
    def _(q):
        at = pl.ds(pl.multiple_of(q * 256, 256), 256)
        rhs_out[at, :] = mm(tt_out[at, :], dem[...])


def front(lf, links, usage, dem):
    n, nodes, arcs = links.shape
    k = n * nodes
    return pl.pallas_call(
        front_kernel,
        out_shape=(
            jax.ShapeDtypeStruct((k, arcs), BF16),
            jax.ShapeDtypeStruct((arcs, k), BF16),
            jax.ShapeDtypeStruct((arcs, dem.shape[-1]), F32),
            jax.ShapeDtypeStruct((n, nodes, 256), BF16),
            jax.ShapeDtypeStruct((n, nodes, 256), BF16),
            jax.ShapeDtypeStruct((n, nodes, nodes - 256), BF16),
            jax.ShapeDtypeStruct((n, nodes, nodes - 256), BF16),
        ),
        in_specs=[VM, ANY, VM, VM],
        out_specs=[VM] * 7,
        scratch_shapes=[
            pltpu.VMEM((n, nodes, arcs), F32),
            pltpu.VMEM((n * nodes // 4, 128), F32),
            pltpu.VMEM((n * nodes // 4, 128), F32),
            pltpu.VMEM((n, nodes, 256), F32),
            pltpu.SemaphoreType.DMA((n,)),
        ],
        compiler_params=pltpu.CompilerParams(vmem_limit_bytes=60 * 2**20),
        name="front",
    )(lf, links, usage, dem.reshape(k, -1))


MESH = pl.DeviceIdType.MESH


def middle_kernel(t, tt, rp, damp, s_out, y_out, c_out,
                  near, far, cross, sbuf, r1, m1, r2, m2, r3,
                  a1, a2, a3, b1, b2, ag, rhs16,
                  p0, p1, p2, p3, q1, q2, yg,
                  u_send, u_half, u_got, u_all, c_part, c_send, c_near, c_far,
                  tt_s, tt_r, s1x_s, s1x_r, s1z_s, s1z_r, s2_s, s2_r, s3_s, s3_r,
                  ca_s, ca_r, cb_s, cb_r, cc_s, cc_r, w_s, w_r):
    com, arc = lax.axis_index("com"), lax.axis_index("arc")
    x, z, yh = com // 8, (com // 2) % 4, com % 2
    yl, core = arc // 2, arc % 2
    nearby = yl * 2 + 1 - core
    opposite = (1 - yl) * 2 + core
    diagonal = (1 - yl) * 2 + 1 - core

    def at_x(i):
        return (i * 8 + z * 2 + yh, arc)

    def at_z(i):
        return (x * 8 + i * 2 + yh, arc)

    def other(i, o):
        return (i + o) % 4

    partner = (com, nearby)
    facing = (com, opposite)
    mirror = (x * 8 + z * 2 + 1 - yh, arc)

    barrier = pltpu.get_barrier_semaphore()
    for peer in [at_x(other(x, o)) for o in (1, 2, 3)] + [at_z(other(z, o)) for o in (1, 2, 3)] + [partner, facing, mirror]:
        pl.semaphore_signal(barrier, inc=1, device_id=peer, device_id_type=MESH)
    pl.semaphore_wait(barrier, 9)

    def copy(src, dst, send, recv, peer):
        return pltpu.make_async_remote_copy(src_ref=src, dst_ref=dst, send_sem=send, recv_sem=recv, device_id=peer, device_id_type=MESH)

    firsts, seconds = (x, z), (z, x)
    first_at, second_at = (at_x, at_z), (at_z, at_x)
    pending = []

    def go(c):
        c.start()
        pending.append(c)

    def slab(ref, h, i):
        return ref.at[i, :, :, :, pl.ds(0, 128)] if h == 0 else ref.at[:, i, :, :, pl.ds(128, 128)]

    def rs_first(src, dst, sems, which):
        for h in (0, 1):
            for o in (1, 2, 3):
                p = other(firsts[h], o)
                go(copy(slab(src, h, p), dst.at[h, 3 - o], sems[0].at[which, h, o - 1], sems[1].at[which, h, 3 - o], first_at[h](p)))

    def rs_second(src, one, mine, two, sems, which):
        for h in (0, 1):
            for s in range(3):
                copy(one.at[h, s], one.at[h, s], sems[0].at[which, h, s], sems[1].at[which, h, s], partner).wait_recv()
            own = src[firsts[0], :, :, :, 0:128] if h == 0 else src[:, firsts[1], :, :, 128:256]
            total = own.astype(F32)
            for s in range(3):
                total = total + one[h, s].astype(F32)
            mine[h] = total.astype(mine.dtype)
            for o in (1, 2, 3):
                p = other(seconds[h], o)
                go(copy(mine.at[h, p], two.at[h, 3 - o], sems[2].at[which, h, o - 1], sems[3].at[which, h, 3 - o], second_at[h](p)))

    def rs_third(mine, two, mine2, three, sems, which):
        for h in (0, 1):
            for s in range(3):
                copy(two.at[h, s], two.at[h, s], sems[2].at[which, h, s], sems[3].at[which, h, s], partner).wait_recv()
            total = mine[h, seconds[h]].astype(F32)
            for s in range(3):
                total = total + two[h, s].astype(F32)
            mine2[h] = total.astype(mine2.dtype)
            go(copy(mine2.at[h, 1 - yh], three.at[h], sems[4].at[which, h], sems[5].at[which, h], mirror))

    def rs_done(mine2, three, sems, which, h):
        copy(three.at[h], three.at[h], sems[4].at[which, h], sems[5].at[which, h], mirror).wait_recv()
        return mine2[h, yh].astype(F32) + three[h].astype(F32)

    def ag_first(full, sems, which):
        for h in (0, 1):
            here = full.at[h, firsts[h], seconds[h], yh]
            go(copy(here, here, sems[4].at[which, h], sems[5].at[which, h], mirror))

    def ag_second(full, sems, which):
        for h in (0, 1):
            there = full.at[h, firsts[h], seconds[h], 1 - yh]
            copy(there, there, sems[4].at[which, h], sems[5].at[which, h], mirror).wait_recv()
            here = full.at[h, firsts[h], seconds[h]]
            for o in (1, 2, 3):
                go(copy(here, here, sems[2].at[which, h, o - 1], sems[3].at[which, h, 3 - o], second_at[h](other(seconds[h], o))))

    def ag_third(full, sems, which):
        for h in (0, 1):
            for s in range(3):
                there = full.at[h, firsts[h], other(seconds[h], s + 1)]
                copy(there, there, sems[2].at[which, h, s], sems[3].at[which, h, s], partner).wait_recv()
            here = full.at[h, firsts[h]]
            for o in (1, 2, 3):
                go(copy(here, here, sems[0].at[which, h, o - 1], sems[1].at[which, h, 3 - o], first_at[h](other(firsts[h], o))))

    def ag_done(full, sems, which, out):
        for h in (0, 1):
            for s in range(3):
                there = full.at[h, other(firsts[h], s + 1)]
                copy(there, there, sems[0].at[which, h, s], sems[1].at[which, h, s], partner).wait_recv()
        for i in range(4):
            for j in range(4):
                rows = slice((i * 4 + j) * 64, (i * 4 + j) * 64 + 64)
                out[rows, 0:128] = full[0, i, j].reshape(64, 128)
                out[rows, 128:256] = full[1, j, i].reshape(64, 128)

    sems = (ca_s, ca_r, cb_s, cb_r, cc_s, cc_r)

    def piece(q):
        return pl.ds(pl.multiple_of(q * 32, 32), 32)

    def rows_of(source, block, q):
        @pl.loop(0, 4)
        def _(j):
            cols = pl.ds(pl.multiple_of(j * 256, 256), 256)
            left = source[:, piece(q), :].reshape(256, -1)
            sbuf[block, :, :, piece(q), cols] = mm(left, t[:, cols]).astype(BF16).reshape(4, 2, 32, 256)

    def x_copy(block, q):
        slot = (x + 3 - block) % 4
        return copy(sbuf.at[block, :, :, piece(q), pl.ds(0, 512)], r1.at[0, slot, :, :, piece(q)],
                    s1x_s.at[block, q], s1x_r.at[slot, q], at_x(block))

    def z_copy(block, q, o):
        p = other(z, o)
        return copy(sbuf.at[block, p, :, piece(q), pl.ds(512, 512)], r1.at[1, 3 - o, block, :, piece(q)],
                    s1z_s.at[block, q, o - 1], s1z_r.at[3 - o, block, q], at_z(p))

    def send_rows(block, q):
        for o in (1, 2, 3):
            z_copy(block, q, o).start()

        @pl.when(block != x)
        def _():
            x_copy(block, q).start()

    def fold_first(q):
        for s in range(3):
            there = r1.at[0, s, :, :, piece(q)]
            copy(there, there, s1x_s.at[0, q], s1x_r.at[s, q], partner).wait_recv()

        @pl.loop(0, 4)
        def _(i):
            total = sbuf[x, i, :, piece(q), 0:512].astype(F32)
            for s in range(3):
                total = total + r1[0, s, i, :, piece(q)].astype(F32)
            m1[0, i, :, piece(q)] = total.astype(BF16)

        for o in (1, 2, 3):
            second_copy(0, q, o).start()
        for s in range(3):
            for b in range(4):
                there = r1.at[1, s, b, :, piece(q)]
                copy(there, there, s1z_s.at[0, q, s], s1z_r.at[s, b, q], partner).wait_recv()

        @pl.loop(0, 4)
        def _(i):
            total = sbuf[i, z, :, piece(q), 512:1024].astype(F32)
            for s in range(3):
                total = total + r1[1, s, i, :, piece(q)].astype(F32)
            m1[1, i, :, piece(q)] = total.astype(BF16)

        for o in (1, 2, 3):
            second_copy(1, q, o).start()

    def second_copy(h, q, o):
        p = other(seconds[h], o)
        return copy(m1.at[h, p, :, piece(q)], r2.at[h, 3 - o, :, piece(q)], s2_s.at[h, q, o - 1], s2_r.at[h, 3 - o, q], second_at[h](p))

    def own_sum(h, q, k):
        if h == 0:
            total = sbuf[x, z, k, piece(q), 0:512].astype(F32)
        else:
            total = sbuf[x, z, k, piece(q), 512:1024].astype(F32)
        for s in range(3):
            total = total + r1[h, s, seconds[h], k, piece(q)].astype(F32)
        for s in range(3):
            total = total + r2[h, s, k, piece(q)].astype(F32)
        return total

    def third_copy(h, q):
        return copy(m2.at[h, piece(q)], r3.at[h, piece(q)], s3_s.at[h, q], s3_r.at[h, q], mirror)

    def fold_second(q):
        for h in (0, 1):
            for s in range(3):
                there = r2.at[h, s, :, piece(q)]
                copy(there, there, s2_s.at[h, q, s], s2_r.at[h, s, q], partner).wait_recv()
            m2[h, piece(q)] = own_sum(h, q, 1 - yh).astype(BF16)
            third_copy(h, q).start()

    def fold_third(q):
        for h in (0, 1):
            third_copy(h, q).wait_recv()
            s_out[piece(q), 512 * h:512 * h + 512] = own_sum(h, q, yh) + r3[h, piece(q)].astype(F32)

    rs_first(rp, a1, sems, 0)
    go(copy(tt, near, tt_s.at[0], tt_r.at[0], partner))

    def face_copy(q):
        return copy(tt.at[:, piece(q)], far.at[:, piece(q)], tt_s.at[1 + q], tt_r.at[1 + q], facing)

    def forward_copy(q):
        return copy(far.at[:, piece(q)], cross.at[:, piece(q)], tt_s.at[5 + q], tt_r.at[5 + q], partner)

    go(face_copy(0))
    go(face_copy(1))

    def quarter_rows(source, block, low, high):
        @pl.loop(low, high)
        def _(q):
            rows_of(source, block, q)
            send_rows(block, q)

    quarter_rows(tt, arc, 0, 2)
    rs_second(rp, a1, b1, a2, sems, 0)
    quarter_rows(tt, arc, 2, 4)
    rs_third(b1, a2, b2, a3, sems, 0)
    copy(tt, near, tt_s.at[0], tt_r.at[0], partner).wait_recv()
    quarter_rows(near, nearby, 0, 2)
    for h in (0, 1):
        rhs_sum = rs_done(b2, a3, sems, 0, h)
        b2[h, yh] = rhs_sum
        ag[h, firsts[h], seconds[h], yh] = rhs_sum.astype(BF16)
    ag_first(ag, sems, 1)
    quarter_rows(near, nearby, 2, 3)
    ag_second(ag, sems, 1)
    quarter_rows(near, nearby, 3, 4)
    ag_third(ag, sems, 1)
    ag_done(ag, sems, 1, rhs16)

    half = t.shape[0] // 2
    mine_rows = pl.ds(pl.multiple_of(core * half, half), half)
    other_rows = pl.ds(pl.multiple_of((1 - core) * half, half), half)
    u_send[0] = mm(t[other_rows, :], rhs16[...]).astype(BF16)
    go(copy(u_send.at[0], u_got.at[0], w_s.at[0], w_r.at[0], partner))
    u_half[...] = mm(t[mine_rows, :], rhs16[...])
    copy(u_got.at[0], u_got.at[0], w_s.at[0], w_r.at[0], partner).wait_recv()
    u_half[...] += u_got[0].astype(F32)
    u_send[1] = u_half[...].astype(BF16)
    go(copy(u_send.at[1], u_got.at[1], w_s.at[1], w_r.at[1], facing))
    go(face_copy(2))
    go(face_copy(3))

    def far_rows(q):
        face_copy(q).wait_recv()
        go(forward_copy(q))
        rows_of(far, opposite, q)
        send_rows(opposite, q)

    def cross_rows(q):
        forward_copy(q).wait_recv()
        rows_of(cross, diagonal, q)
        send_rows(diagonal, q)

    far_rows(0)
    cross_rows(0)
    far_rows(1)
    copy(u_got.at[1], u_got.at[1], w_s.at[1], w_r.at[1], facing).wait_recv()
    u_all[core] = (u_half[...] + u_got[1].astype(F32)).astype(BF16)
    go(copy(u_all.at[core], u_all.at[core], w_s.at[2], w_r.at[2], partner))
    cross_rows(1)
    there = u_all.at[1 - core]
    copy(there, there, w_s.at[2], w_r.at[2], partner).wait_recv()

    @pl.loop(0, 8)
    def _(j):
        left = tt[j]
        part = mm(left[:, 0:half], u_all[0]) + mm(left[:, half:], u_all[1])
        p0[j // 2, pl.ds(2 * (j % 2), 2)] = part.astype(BF16).reshape(2, 2, 32, 256)

    rs_first(p0, p1, sems, 2)
    fold_first(0)
    rs_second(p0, p1, q1, p2, sems, 2)
    fold_first(1)
    rs_third(q1, p2, q2, p3, sems, 2)
    fold_second(0)
    for h in (0, 1):
        prod = rs_done(q2, p3, sems, 2, h)
        yg[h, firsts[h], seconds[h], yh] = b2[h, yh] - damp[x, z, yh] * prod
    ag_first(yg, sems, 3)
    fold_second(1)
    ag_second(yg, sems, 3)
    far_rows(2)
    ag_third(yg, sems, 3)
    cross_rows(2)
    ag_done(yg, sems, 3, y_out)

    @pl.loop(0, 4)
    def _(j):
        rows = pl.ds(pl.multiple_of(j * 256, 256), 256)
        left = y_out[rows, :].T.astype(BF16)
        right = tt[pl.ds(2 * j, 2)].reshape(256, -1)
        part = mm(left, right)

        @pl.when(j == 0)
        def _():
            c_part[...] = part.reshape(c_part.shape)

        @pl.when(j > 0)
        def _():
            c_part[...] += part.reshape(c_part.shape)

    c_send[0:2] = c_part[:, 1 - core].astype(BF16)
    go(copy(c_send.at[pl.ds(0, 2)], c_near, w_s.at[3], w_r.at[3], partner))
    fold_first(2)
    copy(c_near, c_near, w_s.at[3], w_r.at[3], partner).wait_recv()
    c_send[2] = (c_part[1 - yl, core] + c_near[1 - yl].astype(F32)).astype(BF16)
    go(copy(c_send.at[2], c_far, w_s.at[4], w_r.at[4], facing))
    far_rows(3)
    cross_rows(3)
    fold_second(2)
    fold_third(0)
    fold_third(1)
    fold_first(3)
    fold_third(2)
    copy(c_far, c_far, w_s.at[4], w_r.at[4], facing).wait_recv()
    c_out[...] = c_part[yl, core] + c_near[yl].astype(F32) + c_far[...].astype(F32)
    fold_second(3)
    fold_third(3)

    for c in pending:
        c.wait_send()

    @pl.loop(0, 4)
    def _(q):
        @pl.loop(0, 4)
        def _(block):
            for o in (1, 2, 3):
                z_copy(block, q, o).wait_send()

            @pl.when(block != x)
            def _():
                x_copy(block, q).wait_send()

        for h in (0, 1):
            for o in (1, 2, 3):
                second_copy(h, q, o).wait_send()
            third_copy(h, q).wait_send()


def middle(t, tt, rhs_part, damping):
    rows, arcs = t.shape
    scen = rhs_part.shape[1]
    V, DMA = pltpu.VMEM, pltpu.SemaphoreType.DMA
    tt = tt.reshape(8, 128, rows)
    return pl.pallas_call(
        middle_kernel,
        out_shape=(
            jax.ShapeDtypeStruct((128, arcs), F32),
            jax.ShapeDtypeStruct((arcs, scen), F32),
            jax.ShapeDtypeStruct((64, rows), F32),
        ),
        in_specs=[VM] * 4,
        out_specs=[VM] * 3,
        scratch_shapes=[
            V((8, 128, rows), BF16), V((8, 128, rows), BF16), V((8, 128, rows), BF16),
            V((4, 4, 2, 128, arcs), BF16),
            V((2, 3, 4, 2, 128, 512), BF16), V((2, 4, 2, 128, 512), BF16),
            V((2, 3, 2, 128, 512), BF16), V((2, 128, 512), BF16), V((2, 128, 512), BF16),
            V((2, 3, 4, 2, 32, 128), F32), V((2, 3, 2, 32, 128), F32), V((2, 32, 128), F32),
            V((2, 4, 2, 32, 128), F32), V((2, 2, 32, 128), F32),
            V((2, 4, 4, 2, 32, 128), BF16), V((arcs, scen), BF16),
            V((4, 4, 2, 32, 256), BF16),
            V((2, 3, 4, 2, 32, 128), BF16), V((2, 3, 2, 32, 128), BF16), V((2, 32, 128), BF16),
            V((2, 4, 2, 32, 128), BF16), V((2, 2, 32, 128), BF16),
            V((2, 4, 4, 2, 32, 128), F32),
            V((2, rows // 2, scen), BF16), V((rows // 2, scen), F32), V((2, rows // 2, scen), BF16),
            V((2, rows // 2, scen), BF16),
            V((2, 2, 64, rows), F32), V((3, 64, rows), BF16), V((2, 64, rows), BF16), V((64, rows), BF16),
            DMA((9,)), DMA((9,)),
            DMA((4, 4)), DMA((3, 4)), DMA((4, 4, 3)), DMA((3, 4, 4)),
            DMA((2, 4, 3)), DMA((2, 3, 4)), DMA((2, 4)), DMA((2, 4)),
            DMA((4, 2, 3)), DMA((4, 2, 3)), DMA((4, 2, 3)), DMA((4, 2, 3)), DMA((4, 2)), DMA((4, 2)),
            DMA((5,)), DMA((5,)),
        ],
        compiler_params=pltpu.CompilerParams(
            vmem_limit_bytes=63 * 2**20, collective_id=0, has_side_effects=True
        ),
        name="middle",
    )(t, tt, rhs_part.reshape(4, 4, 2, 32, scen), damping.reshape(4, 4, 2, 32, 1))


def back_kernel(corr, share, dh, dl, lh, ll, out):
    n, nodes, _ = dh.shape
    blocks = nodes // 256
    for k in range(n):
        done = [None] * blocks
        for b in reversed(range(blocks)):
            at = slice(256 * b, 256 * b + 256)
            full = slice(k * nodes + 256 * b, k * nodes + 256 * b + 256)
            rest = share[:, full].astype(F32) - corr[:, full].astype(F32)
            for e in range(b + 1, blocks):
                s = (k, slice(256 * e, 256 * e + 256), at)
                rest = rest - mm3(done[e], (lh[s], ll[s]))
            x = mm3(halves(rest), (dh[k, at, :], dl[k, at, :]))
            done[b] = halves(x)
            out[:, full] = x


def back(corr, share, dh, dl, lh, ll):
    return pl.pallas_call(
        back_kernel,
        out_shape=jax.ShapeDtypeStruct(share.shape, F32),
        in_specs=[VM] * 6,
        out_specs=VM,
        compiler_params=pltpu.CompilerParams(vmem_limit_bytes=60 * 2**20),
        name="back",
    )(corr, share, dh, dl, lh, ll)


def on_device(lfactor, links, usage, demands, damping):
    n, nodes, arcs = links.shape
    scen = demands.shape[2]
    dem = demands.reshape(n * nodes, scen)
    t, tt, rhs_part, dh, dl, lh, ll = front(lfactor, links, usage, dem)
    schur, y, corr = middle(t, tt, rhs_part, damping)
    part = scen // 4
    share = lax.dynamic_slice_in_dim(dem, lax.axis_index("arc") * part, part, 1).T
    steps = back(corr, share, dh, dl, lh, ll)
    return schur, y, steps.reshape(part, n, nodes).transpose(1, 2, 0)


def solution(mesh):
    return jax.shard_map(
        on_device,
        mesh=mesh,
        in_specs=(P("com"), P("com", None, "arc"), P("com", "arc"), P("com"), P("arc")),
        out_specs=(P("com", "arc"), P("arc"), P("com", None, "arc")),
        check_vma=False,
    )
```

```python
import functools
import jax
import jax.numpy as jnp
from jax import lax
from jax.experimental import pallas as pl
from jax.experimental.pallas import tpu as pltpu
from jax.sharding import PartitionSpec as P

F32, BF16 = jnp.float32, jnp.bfloat16
VM = pl.BlockSpec(memory_space=pltpu.VMEM)
ANY = pl.BlockSpec(memory_space=pl.ANY)


def halves(x):
    high = x.astype(BF16)
    return high, (x - high.astype(F32)).astype(BF16)


def mm(a, b):
    return jnp.dot(a, b, preferred_element_type=F32)


def mm3(a, b):
    return mm(a[0], b[0]) + (mm(a[0], b[1]) + mm(a[1], b[0]))


def front_kernel(lf, links, usage, dem, t_out, tt_out, rhs_out, dh, dl, lh, ll, cbuf, mbuf, xbuf, xinv, sems):
    n, nodes, _ = lf.shape
    tiles = nodes // 128
    rows = n * tiles
    copies = [pltpu.make_async_copy(links.at[k], cbuf.at[k], sems.at[k]) for k in range(n)]
    for c in copies:
        c.start()
    lane = lax.broadcasted_iota(jnp.int32, (32, 128), 1)
    for k in range(n):
        for t in range(tiles):
            acc = jnp.zeros((32, 128), F32)
            for p in range(4):
                part = lf[k, t * 128 + 32 * p:t * 128 + 32 * p + 32, t * 128:t * 128 + 128]
                acc = jnp.where(lane // 32 == p, part, acc)
            mbuf[pl.ds((k * tiles + t) * 32, 32), :] = acc
    seg = lax.broadcasted_iota(jnp.int32, (rows, 128), 1)
    for i in range(32):
        a = mbuf[pl.ds(i, rows, stride=32), :]

        def spread(j):
            out = jnp.broadcast_to(a[:, j:j + 1], (rows, 128))
            for p in range(1, 4):
                out = jnp.where(seg // 32 == p, jnp.broadcast_to(a[:, 32 * p + j:32 * p + j + 1], (rows, 128)), out)
            return out

        acc = jnp.where(seg % 32 == i, 1.0, 0.0).astype(F32)
        for j in range(i):
            acc = acc - spread(j) * xbuf[pl.ds(j, rows, stride=32), :]
        xbuf[pl.ds(i, rows, stride=32), :] = acc / spread(i)
    for k in range(n):
        for t in range(tiles):
            part = xbuf[pl.ds((k * tiles + t) * 32, 32), :]
            for p in range(4):
                at = t * 128 + 32 * p
                here = (t % 2) * 128
                xinv[k, at:at + 32, here:here + 128] = jnp.where(lane // 32 == p, part, 0.0)
                xinv[k, at:at + 32, 128 - here:256 - here] = jnp.zeros((32, 128), F32)

    r = lax.broadcasted_iota(jnp.int32, (256, 256), 0)
    c = lax.broadcasted_iota(jnp.int32, (256, 256), 1)

    @pl.loop(0, nodes // 256)
    def _(b):
        at = pl.multiple_of(b * 256, 256)
        block = [lf[k, pl.ds(at, 256), pl.ds(at, 256)] for k in range(n)]
        inv = [xinv[k, pl.ds(at, 256), :] for k in range(n)]
        for s in (32, 64, 128):
            keep = (r // (2 * s) == c // (2 * s)) & (r // s > c // s)
            for k in range(n):
                x = halves(inv[k])
                y = mm3(x, halves(jnp.where(keep, block[k], 0.0)))
                inv[k] = inv[k] - mm3(halves(y), x)
        for k in range(n):
            dh[k, pl.ds(at, 256), :], dl[k, pl.ds(at, 256), :] = halves(inv[k])

    for k in range(n):
        for b in range(1, nodes // 256):
            for e in range(b):
                s = (k, slice(256 * b, 256 * b + 256), slice(256 * e, 256 * e + 256))
                lh[s], ll[s] = halves(lf[s])
        copies[k].wait()

    width = 512
    arcs = cbuf.shape[2]
    blocks = nodes // 256
    for k in range(n):
        @pl.loop(0, arcs // width)
        def _(q):
            cols = pl.ds(pl.multiple_of(q * width, width), width)
            use = usage[pl.ds(k, 1), cols].astype(F32)
            done = []
            for b in range(blocks):
                rest = cbuf[k, 256 * b:256 * b + 256, cols] * use
                for e in range(b):
                    s = (k, slice(256 * b, 256 * b + 256), slice(256 * e, 256 * e + 256))
                    rest = rest - mm3((lh[s], ll[s]), done[e])
                s = (k, slice(256 * b, 256 * b + 256))
                out = mm3((dh[s], dl[s]), halves(rest))
                done.append(halves(out))
                t_out[k * nodes + 256 * b:k * nodes + 256 * b + 256, cols] = done[b][0]
                tt_out[cols, k * nodes + 256 * b:k * nodes + 256 * b + 256] = out.T.astype(BF16)

    @pl.loop(0, arcs // 256)
    def _(q):
        at = pl.ds(pl.multiple_of(q * 256, 256), 256)
        rhs_out[at, :] = mm(tt_out[at, :], dem[...])


def front(lf, links, usage, dem):
    n, nodes, arcs = links.shape
    k = n * nodes
    return pl.pallas_call(
        front_kernel,
        out_shape=(
            jax.ShapeDtypeStruct((k, arcs), BF16),
            jax.ShapeDtypeStruct((arcs, k), BF16),
            jax.ShapeDtypeStruct((arcs, dem.shape[-1]), F32),
            jax.ShapeDtypeStruct((n, nodes, 256), BF16),
            jax.ShapeDtypeStruct((n, nodes, 256), BF16),
            jax.ShapeDtypeStruct((n, nodes, nodes - 256), BF16),
            jax.ShapeDtypeStruct((n, nodes, nodes - 256), BF16),
        ),
        in_specs=[VM, ANY, VM, VM],
        out_specs=[VM] * 7,
        scratch_shapes=[
            pltpu.VMEM((n, nodes, arcs), F32),
            pltpu.VMEM((n * nodes // 4, 128), F32),
            pltpu.VMEM((n * nodes // 4, 128), F32),
            pltpu.VMEM((n, nodes, 256), F32),
            pltpu.SemaphoreType.DMA((n,)),
        ],
        compiler_params=pltpu.CompilerParams(vmem_limit_bytes=60 * 2**20),
        name="front",
    )(lf, links, usage, dem.reshape(k, -1))


MESH = pl.DeviceIdType.MESH


def middle_kernel(t, tt, rp, damp, s_out, y_out, c_out,
                  near, far, cross, sbuf, r1, m1, r2, m2, r3,
                  a1, a2, a3, b1, b2, ag, rhs16,
                  p0, p1, p2, p3, q1, q2, yg,
                  u_send, u_half, u_got, u_all, c_part, c_send, c_near, c_far,
                  xs, xr, x_s, x_r, tt_s, tt_r, s1x_s, s1x_r, s1z_s, s1z_r, s2_s, s2_r, s3_s, s3_r,
                  ca_s, ca_r, cb_s, cb_r, cc_s, cc_r, w_s, w_r):
    com, arc = lax.axis_index("com"), lax.axis_index("arc")
    x, z, yh = com // 8, (com // 2) % 4, com % 2
    yl, core = arc // 2, arc % 2
    nearby = yl * 2 + 1 - core
    opposite = (1 - yl) * 2 + core
    diagonal = (1 - yl) * 2 + 1 - core

    def at_x(i):
        return (i * 8 + z * 2 + yh, arc)

    def at_z(i):
        return (x * 8 + i * 2 + yh, arc)

    def other(i, o):
        return (i + o) % 4

    partner = (com, nearby)
    facing = (com, opposite)
    mirror = (x * 8 + z * 2 + 1 - yh, arc)

    barrier = pltpu.get_barrier_semaphore()
    for peer in [at_x(other(x, o)) for o in (1, 2, 3)] + [at_z(other(z, o)) for o in (1, 2, 3)] + [partner, facing, mirror]:
        pl.semaphore_signal(barrier, inc=1, device_id=peer, device_id_type=MESH)
    split = x // 2 != yl

    @pl.when(split)
    def _():
        for j in range(8):
            pl.semaphore_signal(barrier, inc=1, device_id=(arc * 8 + j, x), device_id_type=MESH)

    pl.semaphore_wait(barrier, jnp.where(split, 17, 9))

    def copy(src, dst, send, recv, peer):
        return pltpu.make_async_remote_copy(src_ref=src, dst_ref=dst, send_sem=send, recv_sem=recv, device_id=peer, device_id_type=MESH)

    firsts, seconds = (x, z), (z, x)
    first_at, second_at = (at_x, at_z), (at_z, at_x)
    pending = []

    def go(c):
        c.start()
        pending.append(c)

    def slab(ref, h, i):
        return ref.at[i, :, :, :, pl.ds(0, 128)] if h == 0 else ref.at[:, i, :, :, pl.ds(128, 128)]

    def rs_first(src, dst, sems, which):
        for h in (0, 1):
            for o in (1, 2, 3):
                p = other(firsts[h], o)
                go(copy(slab(src, h, p), dst.at[h, 3 - o], sems[0].at[which, h, o - 1], sems[1].at[which, h, 3 - o], first_at[h](p)))

    def rs_second(src, one, mine, two, sems, which):
        for h in (0, 1):
            for s in range(3):
                copy(one.at[h, s], one.at[h, s], sems[0].at[which, h, s], sems[1].at[which, h, s], partner).wait_recv()
            own = src[firsts[0], :, :, :, 0:128] if h == 0 else src[:, firsts[1], :, :, 128:256]
            total = own.astype(F32)
            for s in range(3):
                total = total + one[h, s].astype(F32)
            mine[h] = total.astype(mine.dtype)
            for o in (1, 2, 3):
                p = other(seconds[h], o)
                go(copy(mine.at[h, p], two.at[h, 3 - o], sems[2].at[which, h, o - 1], sems[3].at[which, h, 3 - o], second_at[h](p)))

    def rs_third(mine, two, mine2, three, sems, which):
        for h in (0, 1):
            for s in range(3):
                copy(two.at[h, s], two.at[h, s], sems[2].at[which, h, s], sems[3].at[which, h, s], partner).wait_recv()
            total = mine[h, seconds[h]].astype(F32)
            for s in range(3):
                total = total + two[h, s].astype(F32)
            mine2[h] = total.astype(mine2.dtype)
            go(copy(mine2.at[h, 1 - yh], three.at[h], sems[4].at[which, h], sems[5].at[which, h], mirror))

    def rs_done(mine2, three, sems, which, h):
        copy(three.at[h], three.at[h], sems[4].at[which, h], sems[5].at[which, h], mirror).wait_recv()
        return mine2[h, yh].astype(F32) + three[h].astype(F32)

    def ag_first(full, sems, which):
        for h in (0, 1):
            here = full.at[h, firsts[h], seconds[h], yh]
            go(copy(here, here, sems[4].at[which, h], sems[5].at[which, h], mirror))

    def ag_second(full, sems, which):
        for h in (0, 1):
            there = full.at[h, firsts[h], seconds[h], 1 - yh]
            copy(there, there, sems[4].at[which, h], sems[5].at[which, h], mirror).wait_recv()
            here = full.at[h, firsts[h], seconds[h]]
            for o in (1, 2, 3):
                go(copy(here, here, sems[2].at[which, h, o - 1], sems[3].at[which, h, 3 - o], second_at[h](other(seconds[h], o))))

    def ag_third(full, sems, which):
        for h in (0, 1):
            for s in range(3):
                there = full.at[h, firsts[h], other(seconds[h], s + 1)]
                copy(there, there, sems[2].at[which, h, s], sems[3].at[which, h, s], partner).wait_recv()
            here = full.at[h, firsts[h]]
            for o in (1, 2, 3):
                go(copy(here, here, sems[0].at[which, h, o - 1], sems[1].at[which, h, 3 - o], first_at[h](other(firsts[h], o))))

    def ag_done(full, sems, which, out):
        for h in (0, 1):
            for s in range(3):
                there = full.at[h, other(firsts[h], s + 1)]
                copy(there, there, sems[0].at[which, h, s], sems[1].at[which, h, s], partner).wait_recv()
        for i in range(4):
            for j in range(4):
                rows = slice((i * 4 + j) * 64, (i * 4 + j) * 64 + 64)
                out[rows, 0:128] = full[0, i, j].astype(out.dtype).reshape(64, 128)
                out[rows, 128:256] = full[1, j, i].astype(out.dtype).reshape(64, 128)

    sems = (ca_s, ca_r, cb_s, cb_r, cc_s, cc_r)

    def piece(q):
        return pl.ds(pl.multiple_of(q * 32, 32), 32)

    half = t.shape[0] // 2
    given = pl.ds(pl.multiple_of(yl * half, half), half)
    taken = pl.ds(pl.multiple_of((1 - yl) * half, half), half)

    def rows_of(source, block, q):
        whole = source.shape[2] == 2 * half

        @pl.loop(0, 4)
        def _(j):
            cols = pl.ds(pl.multiple_of(j * 256, 256), 256)
            left = source[:, piece(q), :].reshape(256, -1)
            sbuf[block, :, :, piece(q), cols] = mm(left, t[:, cols] if whole else t[taken, cols]).astype(BF16).reshape(4, 2, 32, 256)

    def x_copy(block, q):
        slot = (x + 3 - block) % 4
        return copy(sbuf.at[block, :, :, piece(q), pl.ds(0, 512)], r1.at[0, slot, :, :, piece(q)],
                    s1x_s.at[block, q], s1x_r.at[slot, q], at_x(block))

    def z_copy(block, q, o):
        p = other(z, o)
        return copy(sbuf.at[block, p, :, piece(q), pl.ds(512, 512)], r1.at[1, 3 - o, block, :, piece(q)],
                    s1z_s.at[block, q, o - 1], s1z_r.at[3 - o, block, q], at_z(p))

    def send_rows(block, q):
        for o in (1, 2, 3):
            z_copy(block, q, o).start()

        @pl.when(block != x)
        def _():
            x_copy(block, q).start()

    def fold_first(q):
        for s in range(3):
            there = r1.at[0, s, :, :, piece(q)]
            copy(there, there, s1x_s.at[0, q], s1x_r.at[s, q], partner).wait_recv()

        @pl.loop(0, 4)
        def _(i):
            total = sbuf[x, i, :, piece(q), 0:512].astype(F32)
            for s in range(3):
                total = total + r1[0, s, i, :, piece(q)].astype(F32)
            m1[0, i, :, piece(q)] = total.astype(BF16)

        for o in (1, 2, 3):
            second_copy(0, q, o).start()
        for s in range(3):
            for b in range(4):
                there = r1.at[1, s, b, :, piece(q)]
                copy(there, there, s1z_s.at[0, q, s], s1z_r.at[s, b, q], partner).wait_recv()

        @pl.loop(0, 4)
        def _(i):
            total = sbuf[i, z, :, piece(q), 512:1024].astype(F32)
            for s in range(3):
                total = total + r1[1, s, i, :, piece(q)].astype(F32)
            m1[1, i, :, piece(q)] = total.astype(BF16)

        for o in (1, 2, 3):
            second_copy(1, q, o).start()

    def second_copy(h, q, o):
        p = other(seconds[h], o)
        return copy(m1.at[h, p, :, piece(q)], r2.at[h, 3 - o, :, piece(q)], s2_s.at[h, q, o - 1], s2_r.at[h, 3 - o, q], second_at[h](p))

    def own_sum(h, q, k):
        if h == 0:
            total = sbuf[x, z, k, piece(q), 0:512].astype(F32)
        else:
            total = sbuf[x, z, k, piece(q), 512:1024].astype(F32)
        for s in range(3):
            total = total + r1[h, s, seconds[h], k, piece(q)].astype(F32)
        for s in range(3):
            total = total + r2[h, s, k, piece(q)].astype(F32)
        return total

    def third_copy(h, q):
        return copy(m2.at[h, piece(q)], r3.at[h, piece(q)], s3_s.at[h, q], s3_r.at[h, q], mirror)

    def fold_second(q):
        for h in (0, 1):
            for s in range(3):
                there = r2.at[h, s, :, piece(q)]
                copy(there, there, s2_s.at[h, q, s], s2_r.at[h, s, q], partner).wait_recv()
            m2[h, piece(q)] = own_sum(h, q, 1 - yh).astype(BF16)
            third_copy(h, q).start()

    def fold_third(q):
        for h in (0, 1):
            third_copy(h, q).wait_recv()
            s_out[piece(q), 512 * h:512 * h + 512] = own_sum(h, q, yh) + r3[h, piece(q)].astype(F32)

    rs_first(rp, a1, sems, 0)
    go(copy(tt, near, tt_s.at[0], tt_r.at[0], partner))

    def face_copy(q):
        return copy(tt.at[:, piece(q), given], far.at[:, piece(q)], tt_s.at[1 + q], tt_r.at[1 + q], facing)

    def forward_copy(q):
        return copy(far.at[:, piece(q)], cross.at[:, piece(q)], tt_s.at[5 + q], tt_r.at[5 + q], partner)

    def compute_rows(source, block, low, high):
        @pl.loop(low, high)
        def _(q):
            rows_of(source, block, q)

    def far_rows(q):
        face_copy(q).wait_recv()
        go(forward_copy(q))
        rows_of(far, opposite, q)

    def cross_rows(q):
        forward_copy(q).wait_recv()
        rows_of(cross, diagonal, q)

    go(face_copy(0))
    compute_rows(tt, arc, 0, 4)
    rs_second(rp, a1, b1, a2, sems, 0)
    copy(tt, near, tt_s.at[0], tt_r.at[0], partner).wait_recv()
    compute_rows(near, nearby, 0, 2)
    rs_third(b1, a2, b2, a3, sems, 0)
    send_rows(arc, 0)
    compute_rows(near, nearby, 2, 3)
    for h in (0, 1):
        rhs_sum = rs_done(b2, a3, sems, 0, h)
        b2[h, yh] = rhs_sum
        ag[h, firsts[h], seconds[h], yh] = rhs_sum.astype(BF16)
    ag_first(ag, sems, 1)
    compute_rows(near, nearby, 3, 4)
    ag_second(ag, sems, 1)
    go(face_copy(1))
    ag_third(ag, sems, 1)
    ag_done(ag, sems, 1, rhs16)
    send_rows(arc, 1)
    send_rows(arc, 2)
    send_rows(nearby, 0)
    send_rows(nearby, 1)

    mine_rows = pl.ds(pl.multiple_of(core * half, half), half)
    other_rows = pl.ds(pl.multiple_of((1 - core) * half, half), half)
    u_send[0] = mm(t[other_rows, :], rhs16[...]).astype(BF16)
    go(copy(u_send.at[0], u_got.at[0], w_s.at[0], w_r.at[0], partner))
    u_half[...] = mm(t[mine_rows, :], rhs16[...])
    copy(u_got.at[0], u_got.at[0], w_s.at[0], w_r.at[0], partner).wait_recv()
    u_half[...] += u_got[0].astype(F32)
    u_send[1] = u_half[...].astype(BF16)
    go(copy(u_send.at[1], u_got.at[1], w_s.at[1], w_r.at[1], facing))
    go(face_copy(2))
    far_rows(0)
    cross_rows(0)
    copy(u_got.at[1], u_got.at[1], w_s.at[1], w_r.at[1], facing).wait_recv()
    u_all[core] = (u_half[...] + u_got[1].astype(F32)).astype(BF16)
    go(copy(u_all.at[core], u_all.at[core], w_s.at[2], w_r.at[2], partner))
    far_rows(1)
    there = u_all.at[1 - core]
    copy(there, there, w_s.at[2], w_r.at[2], partner).wait_recv()

    @pl.loop(0, 8)
    def _(j):
        left = tt[j]
        part = mm(left[:, 0:half], u_all[0]) + mm(left[:, half:], u_all[1])
        p0[j // 2, pl.ds(2 * (j % 2), 2)] = part.astype(BF16).reshape(2, 2, 32, 256)

    rs_first(p0, p1, sems, 2)
    cross_rows(1)
    rs_second(p0, p1, q1, p2, sems, 2)
    rs_third(q1, p2, q2, p3, sems, 2)
    send_rows(opposite, 0)
    for h in (0, 1):
        prod = rs_done(q2, p3, sems, 2, h)
        yg[h, firsts[h], seconds[h], yh] = (b2[h, yh] - damp[x, z, yh] * prod).astype(BF16)
    ag_first(yg, sems, 3)
    send_rows(diagonal, 0)
    ag_second(yg, sems, 3)
    go(face_copy(3))
    far_rows(2)
    ag_third(yg, sems, 3)
    cross_rows(2)
    ag_done(yg, sems, 3, y_out)
    send_rows(opposite, 1)
    send_rows(diagonal, 1)
    send_rows(arc, 3)
    send_rows(opposite, 2)
    send_rows(nearby, 2)
    send_rows(diagonal, 2)
    send_rows(nearby, 3)

    @pl.loop(0, 4)
    def _(j):
        rows = pl.ds(pl.multiple_of(j * 256, 256), 256)
        left = y_out[rows, :].T.astype(BF16)
        right = tt[pl.ds(2 * j, 2)].reshape(256, -1)
        part = mm(left, right)

        @pl.when(j == 0)
        def _():
            c_part[...] = part.reshape(c_part.shape)

        @pl.when(j > 0)
        def _():
            c_part[...] += part.reshape(c_part.shape)

    c_send[0:2] = c_part[:, 1 - core].astype(BF16)
    go(copy(c_send.at[pl.ds(0, 2)], c_near, w_s.at[3], w_r.at[3], partner))
    fold_first(0)
    far_rows(3)
    send_rows(opposite, 3)
    copy(c_near, c_near, w_s.at[3], w_r.at[3], partner).wait_recv()
    c_send[2] = (c_part[1 - yl, core] + c_near[1 - yl].astype(F32)).astype(BF16)
    go(copy(c_send.at[2], c_far, w_s.at[4], w_r.at[4], facing))
    cross_rows(3)
    send_rows(diagonal, 3)
    fold_first(1)
    fold_second(0)
    fold_first(2)
    fold_second(1)
    fold_first(3)
    fold_third(0)
    copy(c_far, c_far, w_s.at[4], w_r.at[4], facing).wait_recv()
    c_out[...] = c_part[yl, core] + c_near[yl].astype(F32) + c_far[...].astype(F32)
    fold_second(2)
    fold_third(1)
    fold_second(3)
    fold_third(2)
    fold_third(3)

    def swap_copy(j, slot):
        return copy(xs.at[j], xr.at[slot], x_s.at[j], x_r.at[slot], (arc * 8 + j, x))

    @pl.when(split)
    def _():
        for j in range(8):
            xs[j] = s_out[:, 128 * j:128 * j + 128].astype(BF16)
        for j in range(8):
            swap_copy(j, z * 2 + yh).start()
        for j in range(8):
            swap_copy(j, j).wait_recv()
            s_out[:, 128 * j:128 * j + 128] += xr[j].astype(F32).T
        for j in range(8):
            swap_copy(j, z * 2 + yh).wait_send()

    for c in pending:
        c.wait_send()

    @pl.loop(0, 4)
    def _(q):
        @pl.loop(0, 4)
        def _(block):
            for o in (1, 2, 3):
                z_copy(block, q, o).wait_send()

            @pl.when(block != x)
            def _():
                x_copy(block, q).wait_send()

        for h in (0, 1):
            for o in (1, 2, 3):
                second_copy(h, q, o).wait_send()
            third_copy(h, q).wait_send()


def middle(t, tt, rhs_part, damping):
    rows, arcs = t.shape
    scen = rhs_part.shape[1]
    V, DMA = pltpu.VMEM, pltpu.SemaphoreType.DMA
    tt = tt.reshape(8, 128, rows)
    return pl.pallas_call(
        middle_kernel,
        out_shape=(
            jax.ShapeDtypeStruct((128, arcs), F32),
            jax.ShapeDtypeStruct((arcs, scen), F32),
            jax.ShapeDtypeStruct((64, rows), F32),
        ),
        in_specs=[VM] * 4,
        out_specs=[VM] * 3,
        scratch_shapes=[
            V((8, 128, rows), BF16), V((8, 128, rows // 2), BF16), V((8, 128, rows // 2), BF16),
            V((4, 4, 2, 128, arcs), BF16),
            V((2, 3, 4, 2, 128, 512), BF16), V((2, 4, 2, 128, 512), BF16),
            V((2, 3, 2, 128, 512), BF16), V((2, 128, 512), BF16), V((2, 128, 512), BF16),
            V((2, 3, 4, 2, 32, 128), F32), V((2, 3, 2, 32, 128), F32), V((2, 32, 128), F32),
            V((2, 4, 2, 32, 128), F32), V((2, 2, 32, 128), F32),
            V((2, 4, 4, 2, 32, 128), BF16), V((arcs, scen), BF16),
            V((4, 4, 2, 32, 256), BF16),
            V((2, 3, 4, 2, 32, 128), BF16), V((2, 3, 2, 32, 128), BF16), V((2, 32, 128), BF16),
            V((2, 4, 2, 32, 128), BF16), V((2, 2, 32, 128), BF16),
            V((2, 4, 4, 2, 32, 128), BF16),
            V((2, rows // 2, scen), BF16), V((rows // 2, scen), F32), V((2, rows // 2, scen), BF16),
            V((2, rows // 2, scen), BF16),
            V((2, 2, 64, rows), F32), V((3, 64, rows), BF16), V((2, 64, rows), BF16), V((64, rows), BF16),
            V((8, 128, 128), BF16), V((8, 128, 128), BF16), DMA((8,)), DMA((8,)),
            DMA((9,)), DMA((9,)),
            DMA((4, 4)), DMA((3, 4)), DMA((4, 4, 3)), DMA((3, 4, 4)),
            DMA((2, 4, 3)), DMA((2, 3, 4)), DMA((2, 4)), DMA((2, 4)),
            DMA((4, 2, 3)), DMA((4, 2, 3)), DMA((4, 2, 3)), DMA((4, 2, 3)), DMA((4, 2)), DMA((4, 2)),
            DMA((5,)), DMA((5,)),
        ],
        compiler_params=pltpu.CompilerParams(
            vmem_limit_bytes=63 * 2**20, collective_id=0, has_side_effects=True
        ),
        name="middle",
    )(t, tt, rhs_part.reshape(4, 4, 2, 32, scen), damping.reshape(4, 4, 2, 32, 1))


def back_kernel(corr, share, dh, dl, lh, ll, out):
    n, nodes, _ = dh.shape
    blocks = nodes // 256
    for k in range(n):
        done = [None] * blocks
        for b in reversed(range(blocks)):
            at = slice(256 * b, 256 * b + 256)
            full = slice(k * nodes + 256 * b, k * nodes + 256 * b + 256)
            rest = share[:, full].astype(F32) - corr[:, full].astype(F32)
            for e in range(b + 1, blocks):
                s = (k, slice(256 * e, 256 * e + 256), at)
                rest = rest - mm3(done[e], (lh[s], ll[s]))
            x = mm3(halves(rest), (dh[k, at, :], dl[k, at, :]))
            done[b] = halves(x)
            out[:, full] = x


def back(corr, share, dh, dl, lh, ll):
    return pl.pallas_call(
        back_kernel,
        out_shape=jax.ShapeDtypeStruct(share.shape, F32),
        in_specs=[VM] * 6,
        out_specs=VM,
        compiler_params=pltpu.CompilerParams(vmem_limit_bytes=60 * 2**20),
        name="back",
    )(corr, share, dh, dl, lh, ll)


def on_device(lfactor, links, usage, demands, damping):
    n, nodes, arcs = links.shape
    scen = demands.shape[2]
    dem = demands.reshape(n * nodes, scen)
    t, tt, rhs_part, dh, dl, lh, ll = front(lfactor, links, usage, dem)
    schur, y, corr = middle(t, tt, rhs_part, damping)
    part = scen // 4
    share = lax.dynamic_slice_in_dim(dem, lax.axis_index("arc") * part, part, 1).T
    steps = back(corr, share, dh, dl, lh, ll)
    return schur, y, steps.reshape(part, n, nodes).transpose(1, 2, 0)


def solution(mesh):
    return jax.shard_map(
        on_device,
        mesh=mesh,
        in_specs=(P("com"), P("com", None, "arc"), P("com", "arc"), P("com"), P("arc")),
        out_specs=(P("com", "arc"), P("arc"), P("com", None, "arc")),
        check_vma=False,
    )
```

```python
import functools
import jax
import jax.numpy as jnp
from jax import lax
from jax.experimental import pallas as pl
from jax.experimental.pallas import tpu as pltpu
from jax.sharding import PartitionSpec as P

F32, BF16 = jnp.float32, jnp.bfloat16
VM = pl.BlockSpec(memory_space=pltpu.VMEM)
ANY = pl.BlockSpec(memory_space=pl.ANY)


def halves(x):
    high = x.astype(BF16)
    return high, (x - high.astype(F32)).astype(BF16)


def mm(a, b):
    return jnp.dot(a, b, preferred_element_type=F32)


def mm3(a, b):
    return mm(a[0], b[0]) + (mm(a[0], b[1]) + mm(a[1], b[0]))


def front_kernel(lf, links, usage, dem, t_hbm, tt_hbm, rhs_hbm, dh_hbm, dl_hbm, lh_hbm, ll_hbm,
                 t_out, tt_out, rhs_out, dh, dl, lh, ll, cbuf, mbuf, xbuf, xinv, sems, out_sems):
    n, nodes, _ = lf.shape
    tiles = nodes // 128
    rows = n * tiles
    copies = [pltpu.make_async_copy(links.at[k], cbuf.at[k], sems.at[k]) for k in range(n)]
    for c in copies:
        c.start()
    lane = lax.broadcasted_iota(jnp.int32, (32, 128), 1)
    for k in range(n):
        for t in range(tiles):
            acc = jnp.zeros((32, 128), F32)
            for p in range(4):
                part = lf[k, t * 128 + 32 * p:t * 128 + 32 * p + 32, t * 128:t * 128 + 128]
                acc = jnp.where(lane // 32 == p, part, acc)
            mbuf[pl.ds((k * tiles + t) * 32, 32), :] = acc
    seg = lax.broadcasted_iota(jnp.int32, (rows, 128), 1)
    for i in range(32):
        a = mbuf[pl.ds(i, rows, stride=32), :]

        def spread(j):
            out = jnp.broadcast_to(a[:, j:j + 1], (rows, 128))
            for p in range(1, 4):
                out = jnp.where(seg // 32 == p, jnp.broadcast_to(a[:, 32 * p + j:32 * p + j + 1], (rows, 128)), out)
            return out

        acc = jnp.where(seg % 32 == i, 1.0, 0.0).astype(F32)
        for j in range(i):
            acc = acc - spread(j) * xbuf[pl.ds(j, rows, stride=32), :]
        xbuf[pl.ds(i, rows, stride=32), :] = acc / spread(i)
    for k in range(n):
        for t in range(tiles):
            part = xbuf[pl.ds((k * tiles + t) * 32, 32), :]
            for p in range(4):
                at = t * 128 + 32 * p
                here = (t % 2) * 128
                xinv[k, at:at + 32, here:here + 128] = jnp.where(lane // 32 == p, part, 0.0)
                xinv[k, at:at + 32, 128 - here:256 - here] = jnp.zeros((32, 128), F32)

    r = lax.broadcasted_iota(jnp.int32, (256, 256), 0)
    c = lax.broadcasted_iota(jnp.int32, (256, 256), 1)

    @pl.loop(0, nodes // 256)
    def _(b):
        at = pl.multiple_of(b * 256, 256)
        block = [lf[k, pl.ds(at, 256), pl.ds(at, 256)] for k in range(n)]
        inv = [xinv[k, pl.ds(at, 256), :] for k in range(n)]
        for s in (32, 64, 128):
            keep = (r // (2 * s) == c // (2 * s)) & (r // s > c // s)
            for k in range(n):
                x = halves(inv[k])
                y = mm3(x, halves(jnp.where(keep, block[k], 0.0)))
                inv[k] = inv[k] - mm3(halves(y), x)
        for k in range(n):
            dh[k, pl.ds(at, 256), :], dl[k, pl.ds(at, 256), :] = halves(inv[k])

    for k in range(n):
        for b in range(1, nodes // 256):
            for e in range(b):
                s = (k, slice(256 * b, 256 * b + 256), slice(256 * e, 256 * e + 256))
                lh[s], ll[s] = halves(lf[s])
        copies[k].wait()
    leaving = []

    def leave(src, dst):
        leaving.append(pltpu.make_async_copy(src, dst, out_sems.at[len(leaving)]))
        leaving[-1].start()

    for src, dst in ((dh, dh_hbm), (dl, dl_hbm), (lh, lh_hbm), (ll, ll_hbm)):
        leave(src, dst)
    width = 512
    arcs = cbuf.shape[2]
    blocks = nodes // 256
    for k in range(n):
        @pl.loop(0, arcs // width)
        def _(q):
            cols = pl.ds(pl.multiple_of(q * width, width), width)
            use = usage[pl.ds(k, 1), cols].astype(F32)
            done = []
            for b in range(blocks):
                rest = cbuf[k, 256 * b:256 * b + 256, cols] * use
                for e in range(b):
                    s = (k, slice(256 * b, 256 * b + 256), slice(256 * e, 256 * e + 256))
                    rest = rest - mm3((lh[s], ll[s]), done[e])
                s = (k, slice(256 * b, 256 * b + 256))
                out = mm3((dh[s], dl[s]), halves(rest))
                done.append(halves(out))
                t_out[k * nodes + 256 * b:k * nodes + 256 * b + 256, cols] = done[b][0]
                tt_out[cols, k * nodes + 256 * b:k * nodes + 256 * b + 256] = out.T.astype(BF16)

        mine = pl.ds(k * nodes, nodes)
        leave(t_out.at[mine], t_hbm.at[mine])
        leave(tt_out.at[:, mine], tt_hbm.at[:, mine])

    @pl.loop(0, arcs // 256)
    def _(q):
        at = pl.ds(pl.multiple_of(q * 256, 256), 256)
        rhs_out[at, :] = mm(tt_out[at, :], dem[...])

    leave(rhs_out, rhs_hbm)
    for c in leaving:
        c.wait()


def front(lf, links, usage, dem):
    n, nodes, arcs = links.shape
    k = n * nodes
    shapes = (
            jax.ShapeDtypeStruct((k, arcs), BF16),
            jax.ShapeDtypeStruct((arcs, k), BF16),
            jax.ShapeDtypeStruct((arcs, dem.shape[-1]), F32),
            jax.ShapeDtypeStruct((n, nodes, 256), BF16),
            jax.ShapeDtypeStruct((n, nodes, 256), BF16),
            jax.ShapeDtypeStruct((n, nodes, nodes - 256), BF16),
            jax.ShapeDtypeStruct((n, nodes, nodes - 256), BF16),
    )
    return pl.pallas_call(
        front_kernel,
        out_shape=shapes,
        in_specs=[VM, ANY, VM, VM],
        out_specs=[ANY] * 7,
        scratch_shapes=[pltpu.VMEM(a.shape, a.dtype) for a in shapes] + [
            pltpu.VMEM((n, nodes, arcs), F32),
            pltpu.VMEM((n * nodes // 4, 128), F32),
            pltpu.VMEM((n * nodes // 4, 128), F32),
            pltpu.VMEM((n, nodes, 256), F32),
            pltpu.SemaphoreType.DMA((n,)),
            pltpu.SemaphoreType.DMA((5 + 2 * n,)),
        ],
        compiler_params=pltpu.CompilerParams(vmem_limit_bytes=60 * 2**20),
        name="front",
    )(lf, links, usage, dem.reshape(k, -1))


MESH = pl.DeviceIdType.MESH


def upper_solve(corr, share, dh, dl, lh, ll, out):
    n, nodes, _ = dh.shape
    blocks = nodes // 256
    for k in range(n):
        done = [None] * blocks
        for b in reversed(range(blocks)):
            at = slice(256 * b, 256 * b + 256)
            full = slice(k * nodes + 256 * b, k * nodes + 256 * b + 256)
            rest = share[:, full].astype(F32) - corr[:, full].astype(F32)
            for e in range(b + 1, blocks):
                s = (k, slice(256 * e, 256 * e + 256), at)
                rest = rest - mm3(done[e], (lh[s], ll[s]))
            x = mm3(halves(rest), (dh[k, at, :], dl[k, at, :]))
            done[b] = halves(x)
            out[k, at, :] = x.T


def middle_kernel(damp, t_in, tt_in, rp_in, dem_in, dh_in, dl_in, lh_in, ll_in, s_out, y_out, st_out, c_out,
                  t, tt, rp, dm, dmt, dh, dl, lh, ll, in_s,
                  near, far, cross, sbuf, r1, mb, m1, r2, m2, r3,
                  a1, a2, a3, b1, b2, ag, rhs16,
                  p0, p1, p2, p3, q1, q2, yg,
                  u_send, u_half, u_got, u_all, c_part, c_send, c_near, c_far,
                  xs, xr, x_s, x_r, tt_s, tt_r, s1x_s, s1x_r, s1z_s, s1z_r, sb_s, sb_r, s2_s, s2_r, s3_s, s3_r,
                  ca_s, ca_r, cb_s, cb_r, cc_s, cc_r, w_s, w_r):
    com, arc = lax.axis_index("com"), lax.axis_index("arc")
    x, z, yh = com // 8, (com // 2) % 4, com % 2
    yl, core = arc // 2, arc % 2
    nearby = yl * 2 + 1 - core
    opposite = (1 - yl) * 2 + core
    diagonal = (1 - yl) * 2 + 1 - core

    def at_x(i):
        return (i * 8 + z * 2 + yh, arc)

    def at_z(i):
        return (x * 8 + i * 2 + yh, arc)

    def other(i, o):
        return (i + o) % 4

    partner = (com, nearby)
    facing = (com, opposite)
    mirror = (x * 8 + z * 2 + 1 - yh, arc)

    loads = [pltpu.make_async_copy(src, dst, in_s.at[i]) for i, (src, dst) in enumerate(
        ((rp_in, rp), (tt_in, tt), (t_in, t), (dem_in, dm), (dh_in, dh), (dl_in, dl), (lh_in, lh), (ll_in, ll)))]
    for c in loads:
        c.start()
    barrier = pltpu.get_barrier_semaphore()
    for peer in [at_x(other(x, o)) for o in (1, 2, 3)] + [at_z(other(z, o)) for o in (1, 2, 3)] + [partner, facing, mirror]:
        pl.semaphore_signal(barrier, inc=1, device_id=peer, device_id_type=MESH)
    split = x // 2 != yl

    @pl.when(split)
    def _():
        for j in range(8):
            pl.semaphore_signal(barrier, inc=1, device_id=(arc * 8 + j, x), device_id_type=MESH)

    pl.semaphore_wait(barrier, jnp.where(split, 17, 9))

    def copy(src, dst, send, recv, peer):
        return pltpu.make_async_remote_copy(src_ref=src, dst_ref=dst, send_sem=send, recv_sem=recv, device_id=peer, device_id_type=MESH)

    firsts, seconds = (x, z), (z, x)
    first_at, second_at = (at_x, at_z), (at_z, at_x)
    pending = []

    def go(c):
        c.start()
        pending.append(c)

    def slab(ref, h, i):
        return ref.at[i, :, :, :, pl.ds(0, 128)] if h == 0 else ref.at[:, i, :, :, pl.ds(128, 128)]

    def rs_first(src, dst, sems, which):
        for h in (0, 1):
            for o in (1, 2, 3):
                p = other(firsts[h], o)
                go(copy(slab(src, h, p), dst.at[h, 3 - o], sems[0].at[which, h, o - 1], sems[1].at[which, h, 3 - o], first_at[h](p)))

    def rs_second(src, one, mine, two, sems, which):
        for h in (0, 1):
            for s in range(3):
                copy(one.at[h, s], one.at[h, s], sems[0].at[which, h, s], sems[1].at[which, h, s], partner).wait_recv()
            own = src[firsts[0], :, :, :, 0:128] if h == 0 else src[:, firsts[1], :, :, 128:256]
            total = own.astype(F32)
            for s in range(3):
                total = total + one[h, s].astype(F32)
            mine[h] = total.astype(mine.dtype)
            for o in (1, 2, 3):
                p = other(seconds[h], o)
                go(copy(mine.at[h, p], two.at[h, 3 - o], sems[2].at[which, h, o - 1], sems[3].at[which, h, 3 - o], second_at[h](p)))

    def rs_third(mine, two, mine2, three, sems, which):
        for h in (0, 1):
            for s in range(3):
                copy(two.at[h, s], two.at[h, s], sems[2].at[which, h, s], sems[3].at[which, h, s], partner).wait_recv()
            total = mine[h, seconds[h]].astype(F32)
            for s in range(3):
                total = total + two[h, s].astype(F32)
            mine2[h] = total.astype(mine2.dtype)
            go(copy(mine2.at[h, 1 - yh], three.at[h], sems[4].at[which, h], sems[5].at[which, h], mirror))

    def rs_done(mine2, three, sems, which, h):
        copy(three.at[h], three.at[h], sems[4].at[which, h], sems[5].at[which, h], mirror).wait_recv()
        return mine2[h, yh].astype(F32) + three[h].astype(F32)

    def ag_first(full, sems, which):
        for h in (0, 1):
            here = full.at[h, firsts[h], seconds[h], yh]
            go(copy(here, here, sems[4].at[which, h], sems[5].at[which, h], mirror))

    def ag_second(full, sems, which):
        for h in (0, 1):
            there = full.at[h, firsts[h], seconds[h], 1 - yh]
            copy(there, there, sems[4].at[which, h], sems[5].at[which, h], mirror).wait_recv()
            here = full.at[h, firsts[h], seconds[h]]
            for o in (1, 2, 3):
                go(copy(here, here, sems[2].at[which, h, o - 1], sems[3].at[which, h, 3 - o], second_at[h](other(seconds[h], o))))

    def ag_third(full, sems, which):
        for h in (0, 1):
            for s in range(3):
                there = full.at[h, firsts[h], other(seconds[h], s + 1)]
                copy(there, there, sems[2].at[which, h, s], sems[3].at[which, h, s], partner).wait_recv()
            here = full.at[h, firsts[h]]
            for o in (1, 2, 3):
                go(copy(here, here, sems[0].at[which, h, o - 1], sems[1].at[which, h, 3 - o], first_at[h](other(firsts[h], o))))

    def ag_done(full, sems, which, out):
        for h in (0, 1):
            for s in range(3):
                there = full.at[h, other(firsts[h], s + 1)]
                copy(there, there, sems[0].at[which, h, s], sems[1].at[which, h, s], partner).wait_recv()
        for i in range(4):
            for j in range(4):
                rows = slice((i * 4 + j) * 64, (i * 4 + j) * 64 + 64)
                out[rows, 0:128] = full[0, i, j].astype(out.dtype).reshape(64, 128)
                out[rows, 128:256] = full[1, j, i].astype(out.dtype).reshape(64, 128)

    sems = (ca_s, ca_r, cb_s, cb_r, cc_s, cc_r)

    def piece(q):
        return pl.ds(pl.multiple_of(q * 32, 32), 32)

    half = t.shape[0] // 2
    given = pl.ds(pl.multiple_of(yl * half, half), half)
    taken = pl.ds(pl.multiple_of((1 - yl) * half, half), half)

    def rows_of(source, block, q):
        whole = source.shape[2] == 2 * half

        @pl.loop(0, 4)
        def _(j):
            cols = pl.ds(pl.multiple_of(j * 256, 256), 256)
            left = source[:, piece(q), :].reshape(256, -1)
            sbuf[block, :, :, piece(q), cols] = mm(left, t[:, cols] if whole else t[taken, cols]).astype(BF16).reshape(4, 2, 32, 256)

    def flip(i):
        return i + 1 - 2 * (i % 2)

    def turn(i):
        return 3 - i

    def ways(q):
        return (flip, turn) if q % 2 == 0 else (turn, flip)

    def x_copy(q, s):
        one, two = ways(q)
        block = one(x) if s == 0 else two(one(x))
        return block, copy(sbuf.at[block, :, :, piece(q), pl.ds(0, 512)], r1.at[0, s, :, :, piece(q)],
                           s1x_s.at[s, q], s1x_r.at[s, q], at_x(one(x)))

    def z_copy(block, q, s):
        one, two = ways(q)
        part = one(z) if s == 0 else two(one(z))
        return copy(sbuf.at[block, part, :, piece(q), pl.ds(512, 512)], r1.at[1, s, block, :, piece(q)],
                    s1z_s.at[s, block, q], s1z_r.at[s, block, q], at_z(one(z)))

    def relay_copy(h, q):
        two = ways(q)[1]
        return copy(mb.at[h, :, :, piece(q)], r1.at[h, 2, :, :, piece(q)], sb_s.at[h, q], sb_r.at[h, q], first_at[h](two(firsts[h])))

    def send_rows(block, q):
        for s in (1, 0):
            z_copy(block, q, s).start()
            wanted, c = x_copy(q, s)
            pl.when(block == wanted)(c.start)

    def fold_zero(q):
        two = ways(q)[1]
        x_copy(q, 1)[1].wait_recv()

        @pl.loop(0, 4)
        def _(i):
            mb[0, i, :, piece(q)] = (sbuf[two(x), i, :, piece(q), 0:512].astype(F32) + r1[0, 1, i, :, piece(q)].astype(F32)).astype(BF16)

        relay_copy(0, q).start()
        for b in range(4):
            z_copy(b, q, 1).wait_recv()

        @pl.loop(0, 4)
        def _(i):
            mb[1, i, :, piece(q)] = (sbuf[i, two(z), :, piece(q), 512:1024].astype(F32) + r1[1, 1, i, :, piece(q)].astype(F32)).astype(BF16)

        relay_copy(1, q).start()

    def fold_first(q):
        x_copy(q, 0)[1].wait_recv()
        for b in range(4):
            z_copy(b, q, 0).wait_recv()
        for h in (0, 1):
            relay_copy(h, q).wait_recv()

            @pl.loop(0, 4)
            def _(i):
                own = sbuf[x, i, :, piece(q), 0:512] if h == 0 else sbuf[i, z, :, piece(q), 512:1024]
                total = own.astype(F32) + r1[h, 0, i, :, piece(q)].astype(F32) + r1[h, 2, i, :, piece(q)].astype(F32)
                m1[h, i, :, piece(q)] = total.astype(BF16)

            for o in (1, 2, 3):
                second_copy(h, q, o).start()

    def second_copy(h, q, o):
        p = other(seconds[h], o)
        return copy(m1.at[h, p, :, piece(q)], r2.at[h, 3 - o, :, piece(q)], s2_s.at[h, q, o - 1], s2_r.at[h, 3 - o, q], second_at[h](p))

    def own_sum(h, q, k):
        if h == 0:
            total = sbuf[x, z, k, piece(q), 0:512].astype(F32)
        else:
            total = sbuf[x, z, k, piece(q), 512:1024].astype(F32)
        for s in (0, 2):
            total = total + r1[h, s, seconds[h], k, piece(q)].astype(F32)
        for s in range(3):
            total = total + r2[h, s, k, piece(q)].astype(F32)
        return total

    def third_copy(h, q):
        return copy(m2.at[h, piece(q)], r3.at[h, piece(q)], s3_s.at[h, q], s3_r.at[h, q], mirror)

    def fold_second(q):
        for h in (0, 1):
            for s in range(3):
                there = r2.at[h, s, :, piece(q)]
                copy(there, there, s2_s.at[h, q, s], s2_r.at[h, s, q], partner).wait_recv()
            m2[h, piece(q)] = own_sum(h, q, 1 - yh).astype(BF16)
            third_copy(h, q).start()

    def fold_third(q):
        for h in (0, 1):
            third_copy(h, q).wait_recv()
            s_out[piece(q), 512 * h:512 * h + 512] = own_sum(h, q, yh) + r3[h, piece(q)].astype(F32)

    loads[0].wait()
    rs_first(rp, a1, sems, 0)
    loads[1].wait()
    go(copy(tt, near, tt_s.at[0], tt_r.at[0], partner))

    def face_copy(q):
        return copy(tt.at[:, piece(q), given], far.at[:, piece(q)], tt_s.at[1 + q], tt_r.at[1 + q], facing)

    def forward_copy(q):
        return copy(far.at[:, piece(q)], cross.at[:, piece(q)], tt_s.at[5 + q], tt_r.at[5 + q], partner)

    def compute_rows(source, block, low, high):
        @pl.loop(low, high)
        def _(q):
            rows_of(source, block, q)

    def far_rows(q):
        face_copy(q).wait_recv()
        go(forward_copy(q))
        rows_of(far, opposite, q)

    def cross_rows(q):
        forward_copy(q).wait_recv()
        rows_of(cross, diagonal, q)

    go(face_copy(0))
    loads[2].wait()
    compute_rows(tt, arc, 0, 4)
    rs_second(rp, a1, b1, a2, sems, 0)
    copy(tt, near, tt_s.at[0], tt_r.at[0], partner).wait_recv()
    compute_rows(near, nearby, 0, 2)
    rs_third(b1, a2, b2, a3, sems, 0)
    send_rows(arc, 0)
    compute_rows(near, nearby, 2, 3)
    for h in (0, 1):
        rhs_sum = rs_done(b2, a3, sems, 0, h)
        b2[h, yh] = rhs_sum
        ag[h, firsts[h], seconds[h], yh] = rhs_sum.astype(BF16)
    ag_first(ag, sems, 1)
    compute_rows(near, nearby, 3, 4)
    ag_second(ag, sems, 1)
    go(face_copy(1))
    ag_third(ag, sems, 1)
    ag_done(ag, sems, 1, rhs16)
    send_rows(nearby, 0)
    send_rows(arc, 1)
    send_rows(nearby, 1)
    send_rows(arc, 2)
    send_rows(nearby, 2)

    mine_rows = pl.ds(pl.multiple_of(core * half, half), half)
    other_rows = pl.ds(pl.multiple_of((1 - core) * half, half), half)
    u_send[0] = mm(t[other_rows, :], rhs16[...]).astype(BF16)
    go(copy(u_send.at[0], u_got.at[0], w_s.at[0], w_r.at[0], partner))
    u_half[...] = mm(t[mine_rows, :], rhs16[...])
    copy(u_got.at[0], u_got.at[0], w_s.at[0], w_r.at[0], partner).wait_recv()
    u_half[...] += u_got[0].astype(F32)
    u_send[1] = u_half[...].astype(BF16)
    go(copy(u_send.at[1], u_got.at[1], w_s.at[1], w_r.at[1], facing))
    go(face_copy(2))
    far_rows(0)
    cross_rows(0)
    send_rows(arc, 3)
    send_rows(nearby, 3)
    copy(u_got.at[1], u_got.at[1], w_s.at[1], w_r.at[1], facing).wait_recv()
    u_all[core] = (u_half[...] + u_got[1].astype(F32)).astype(BF16)
    go(copy(u_all.at[core], u_all.at[core], w_s.at[2], w_r.at[2], partner))
    far_rows(1)
    there = u_all.at[1 - core]
    copy(there, there, w_s.at[2], w_r.at[2], partner).wait_recv()

    @pl.loop(0, 8)
    def _(j):
        left = tt[j]
        part = mm(left[:, 0:half], u_all[0]) + mm(left[:, half:], u_all[1])
        p0[j // 2, pl.ds(2 * (j % 2), 2)] = part.astype(BF16).reshape(2, 2, 32, 256)

    rs_first(p0, p1, sems, 2)
    cross_rows(1)
    rs_second(p0, p1, q1, p2, sems, 2)
    rs_third(q1, p2, q2, p3, sems, 2)
    send_rows(opposite, 0)
    send_rows(diagonal, 0)
    for h in (0, 1):
        prod = rs_done(q2, p3, sems, 2, h)
        yg[h, firsts[h], seconds[h], yh] = (b2[h, yh] - damp[x, z, yh] * prod).astype(BF16)
    ag_first(yg, sems, 3)
    send_rows(opposite, 1)
    ag_second(yg, sems, 3)
    go(face_copy(3))
    far_rows(2)
    ag_third(yg, sems, 3)
    send_rows(diagonal, 1)
    cross_rows(2)
    fold_zero(0)
    ag_done(yg, sems, 3, y_out)
    send_rows(opposite, 2)
    send_rows(diagonal, 2)

    @pl.loop(0, 4)
    def _(j):
        rows = pl.ds(pl.multiple_of(j * 256, 256), 256)
        left = y_out[rows, :].astype(F32).T.astype(BF16)
        right = tt[pl.ds(2 * j, 2)].reshape(256, -1)
        part = mm(left, right)

        @pl.when(j == 0)
        def _():
            c_part[...] = part.reshape(c_part.shape)

        @pl.when(j > 0)
        def _():
            c_part[...] += part.reshape(c_part.shape)

    c_send[0:2] = c_part[:, 1 - core].astype(BF16)
    go(copy(c_send.at[pl.ds(0, 2)], c_near, w_s.at[3], w_r.at[3], partner))
    fold_zero(1)
    fold_first(0)
    far_rows(3)
    send_rows(opposite, 3)
    copy(c_near, c_near, w_s.at[3], w_r.at[3], partner).wait_recv()
    c_send[2] = (c_part[1 - yl, core] + c_near[1 - yl].astype(F32)).astype(BF16)
    go(copy(c_send.at[2], c_far, w_s.at[4], w_r.at[4], facing))
    cross_rows(3)
    send_rows(diagonal, 3)
    fold_first(1)
    fold_zero(2)
    fold_second(0)
    fold_zero(3)
    fold_second(1)
    fold_first(2)
    fold_third(0)
    fold_first(3)
    fold_third(1)
    copy(c_far, c_far, w_s.at[4], w_r.at[4], facing).wait_recv()
    c_out[...] = c_part[yl, core] + c_near[yl].astype(F32) + c_far[...].astype(F32)
    for c in loads[3:]:
        c.wait()
    for b in range(6):
        dmt[:, 256 * b:256 * b + 256] = dm[256 * b:256 * b + 256, :].astype(F32).T
    upper_solve(c_out, dmt.at[pl.ds(pl.multiple_of(arc * 64, 64), 64)], dh, dl, lh, ll, st_out)
    fold_second(2)
    fold_second(3)
    fold_third(2)
    fold_third(3)

    def swap_copy(j, slot):
        return copy(xs.at[j], xr.at[slot], x_s.at[j], x_r.at[slot], (arc * 8 + j, x))

    @pl.when(split)
    def _():
        for j in range(8):
            xs[j] = s_out[:, 128 * j:128 * j + 128].astype(BF16)
        for j in range(8):
            swap_copy(j, z * 2 + yh).start()
        for j in range(8):
            swap_copy(j, j).wait_recv()
            s_out[:, 128 * j:128 * j + 128] += xr[j].astype(F32).T
        for j in range(8):
            swap_copy(j, z * 2 + yh).wait_send()

    for c in pending:
        c.wait_send()

    for q in range(4):
        for s in (0, 1):
            for block in range(4):
                z_copy(block, q, s).wait_send()
            x_copy(q, s)[1].wait_send()
        for h in (0, 1):
            relay_copy(h, q).wait_send()
        for h in (0, 1):
            for o in (1, 2, 3):
                second_copy(h, q, o).wait_send()
            third_copy(h, q).wait_send()


def middle(t, tt, rhs_part, damping, dem, dh, dl, lh, ll):
    rows, arcs = t.shape
    scen = rhs_part.shape[1]
    V, DMA = pltpu.VMEM, pltpu.SemaphoreType.DMA
    tt = tt.reshape(8, 128, rows)
    return pl.pallas_call(
        middle_kernel,
        out_shape=(
            jax.ShapeDtypeStruct((128, arcs), F32),
            jax.ShapeDtypeStruct((arcs, scen), BF16),
            jax.ShapeDtypeStruct((dh.shape[0], dh.shape[1], 64), F32),
        ),
        in_specs=[VM] + [ANY] * 8,
        out_specs=[VM] * 3,
        scratch_shapes=[
            V((64, rows), F32), V((rows, arcs), BF16), V((8, 128, rows), BF16), V((4, 4, 2, 32, scen), F32),
            V((rows, scen), BF16), V((scen, rows), F32), V(dh.shape, BF16), V(dl.shape, BF16), V(lh.shape, BF16), V(ll.shape, BF16), DMA((8,)),
            V((8, 128, rows), BF16), V((8, 128, rows // 2), BF16), V((8, 128, rows // 2), BF16),
            V((4, 4, 2, 128, arcs), BF16),
            V((2, 3, 4, 2, 128, 512), BF16), V((2, 4, 2, 128, 512), BF16), V((2, 4, 2, 128, 512), BF16),
            V((2, 3, 2, 128, 512), BF16), V((2, 128, 512), BF16), V((2, 128, 512), BF16),
            V((2, 3, 4, 2, 32, 128), F32), V((2, 3, 2, 32, 128), F32), V((2, 32, 128), F32),
            V((2, 4, 2, 32, 128), F32), V((2, 2, 32, 128), F32),
            V((2, 4, 4, 2, 32, 128), BF16), V((arcs, scen), BF16),
            V((4, 4, 2, 32, 256), BF16),
            V((2, 3, 4, 2, 32, 128), BF16), V((2, 3, 2, 32, 128), BF16), V((2, 32, 128), BF16),
            V((2, 4, 2, 32, 128), BF16), V((2, 2, 32, 128), BF16),
            V((2, 4, 4, 2, 32, 128), BF16),
            V((2, rows // 2, scen), BF16), V((rows // 2, scen), F32), V((2, rows // 2, scen), BF16),
            V((2, rows // 2, scen), BF16),
            V((2, 2, 64, rows), F32), V((3, 64, rows), BF16), V((2, 64, rows), BF16), V((64, rows), BF16),
            V((8, 128, 128), BF16), V((8, 128, 128), BF16), DMA((8,)), DMA((8,)),
            DMA((9,)), DMA((9,)),
            DMA((2, 4)), DMA((2, 4)), DMA((2, 4, 4)), DMA((2, 4, 4)), DMA((2, 4)), DMA((2, 4)),
            DMA((2, 4, 3)), DMA((2, 3, 4)), DMA((2, 4)), DMA((2, 4)),
            DMA((4, 2, 3)), DMA((4, 2, 3)), DMA((4, 2, 3)), DMA((4, 2, 3)), DMA((4, 2)), DMA((4, 2)),
            DMA((5,)), DMA((5,)),
        ],
        compiler_params=pltpu.CompilerParams(
            vmem_limit_bytes=63 * 2**20, collective_id=0, has_side_effects=True
        ),
        name="middle",
    )(damping.reshape(4, 4, 2, 32, 1), t, tt, rhs_part.reshape(4, 4, 2, 32, scen), dem, dh, dl, lh, ll)


def on_device(lfactor, links, usage, demands, damping):
    n, nodes, arcs = links.shape
    dem = demands.reshape(n * nodes, demands.shape[2])
    t, tt, rhs_part, dh, dl, lh, ll = front(lfactor, links, usage, dem)
    schur, y, steps = middle(t, tt, rhs_part, damping, dem, dh, dl, lh, ll)
    return schur, y.astype(F32), steps


def solution(mesh):
    return jax.shard_map(
        on_device,
        mesh=mesh,
        in_specs=(P("com"), P("com", None, "arc"), P("com", "arc"), P("com"), P("arc")),
        out_specs=(P("com", "arc"), P("arc"), P("com", None, "arc")),
        check_vma=False,
    )
```

```python
import functools
import jax
import jax.numpy as jnp
from jax import lax
from jax.experimental import pallas as pl
from jax.experimental.pallas import tpu as pltpu
from jax.sharding import PartitionSpec as P

F32, BF16 = jnp.float32, jnp.bfloat16
VM = pl.BlockSpec(memory_space=pltpu.VMEM)
ANY = pl.BlockSpec(memory_space=pl.ANY)


def halves(x):
    high = x.astype(BF16)
    return high, (x - high.astype(F32)).astype(BF16)


def mm(a, b):
    return jnp.dot(a, b, preferred_element_type=F32)


def mm3(a, b):
    return mm(a[0], b[0]) + (mm(a[0], b[1]) + mm(a[1], b[0]))


def front_kernel(lf, links, usage, dem, t_hbm, tt_hbm, rhs_hbm, dh_hbm, dl_hbm, lh_hbm, ll_hbm,
                 t_out, tt_out, rhs_out, dh, dl, lh, ll, cbuf, mbuf, xbuf, xinv, sems, out_sems):
    n, nodes, _ = lf.shape
    tiles = nodes // 128
    rows = n * tiles
    copies = [pltpu.make_async_copy(links.at[k], cbuf.at[k], sems.at[k]) for k in range(n)]
    for c in copies:
        c.start()
    lane = lax.broadcasted_iota(jnp.int32, (32, 128), 1)
    for k in range(n):
        for t in range(tiles):
            acc = jnp.zeros((32, 128), F32)
            for p in range(4):
                part = lf[k, t * 128 + 32 * p:t * 128 + 32 * p + 32, t * 128:t * 128 + 128]
                acc = jnp.where(lane // 32 == p, part, acc)
            mbuf[pl.ds((k * tiles + t) * 32, 32), :] = acc
    seg = lax.broadcasted_iota(jnp.int32, (rows, 128), 1)
    for i in range(32):
        a = mbuf[pl.ds(i, rows, stride=32), :]

        def spread(j):
            out = jnp.broadcast_to(a[:, j:j + 1], (rows, 128))
            for p in range(1, 4):
                out = jnp.where(seg // 32 == p, jnp.broadcast_to(a[:, 32 * p + j:32 * p + j + 1], (rows, 128)), out)
            return out

        acc = jnp.where(seg % 32 == i, 1.0, 0.0).astype(F32)
        for j in range(i):
            acc = acc - spread(j) * xbuf[pl.ds(j, rows, stride=32), :]
        xbuf[pl.ds(i, rows, stride=32), :] = acc / spread(i)
    for k in range(n):
        for t in range(tiles):
            part = xbuf[pl.ds((k * tiles + t) * 32, 32), :]
            for p in range(4):
                at = t * 128 + 32 * p
                here = (t % 2) * 128
                xinv[k, at:at + 32, here:here + 128] = jnp.where(lane // 32 == p, part, 0.0)
                xinv[k, at:at + 32, 128 - here:256 - here] = jnp.zeros((32, 128), F32)

    r = lax.broadcasted_iota(jnp.int32, (256, 256), 0)
    c = lax.broadcasted_iota(jnp.int32, (256, 256), 1)

    @pl.loop(0, nodes // 256)
    def _(b):
        at = pl.multiple_of(b * 256, 256)
        block = [lf[k, pl.ds(at, 256), pl.ds(at, 256)] for k in range(n)]
        inv = [xinv[k, pl.ds(at, 256), :] for k in range(n)]
        for s in (32, 64, 128):
            keep = (r // (2 * s) == c // (2 * s)) & (r // s > c // s)
            for k in range(n):
                x = halves(inv[k])
                y = mm3(x, halves(jnp.where(keep, block[k], 0.0)))
                inv[k] = inv[k] - mm3(halves(y), x)
        for k in range(n):
            dh[k, pl.ds(at, 256), :], dl[k, pl.ds(at, 256), :] = halves(inv[k])

    for k in range(n):
        for b in range(1, nodes // 256):
            for e in range(b):
                s = (k, slice(256 * b, 256 * b + 256), slice(256 * e, 256 * e + 256))
                lh[s], ll[s] = halves(lf[s])
        copies[k].wait()
    leaving = []

    def leave(src, dst):
        leaving.append(pltpu.make_async_copy(src, dst, out_sems.at[len(leaving)]))
        leaving[-1].start()

    for src, dst in ((dh, dh_hbm), (dl, dl_hbm), (lh, lh_hbm), (ll, ll_hbm)):
        leave(src, dst)
    width = 512
    arcs = cbuf.shape[2]
    blocks = nodes // 256
    for k in range(n):
        @pl.loop(0, arcs // width)
        def _(q):
            cols = pl.ds(pl.multiple_of(q * width, width), width)
            use = usage[pl.ds(k, 1), cols].astype(F32)
            done = []
            for b in range(blocks):
                rest = cbuf[k, 256 * b:256 * b + 256, cols] * use
                for e in range(b):
                    s = (k, slice(256 * b, 256 * b + 256), slice(256 * e, 256 * e + 256))
                    rest = rest - mm3((lh[s], ll[s]), done[e])
                s = (k, slice(256 * b, 256 * b + 256))
                out = mm3((dh[s], dl[s]), halves(rest))
                done.append(halves(out))
                t_out[k * nodes + 256 * b:k * nodes + 256 * b + 256, cols] = done[b][0]
                tt_out[cols, k * nodes + 256 * b:k * nodes + 256 * b + 256] = out.T.astype(BF16)

        mine = pl.ds(k * nodes, nodes)
        leave(t_out.at[mine], t_hbm.at[mine])
        leave(tt_out.at[:, mine], tt_hbm.at[:, mine])

    @pl.loop(0, arcs // 256)
    def _(q):
        at = pl.ds(pl.multiple_of(q * 256, 256), 256)
        rhs_out[at, :] = mm(tt_out[at, :], dem[...])

    leave(rhs_out, rhs_hbm)
    for c in leaving:
        c.wait()


def front(lf, links, usage, dem):
    n, nodes, arcs = links.shape
    k = n * nodes
    shapes = (
            jax.ShapeDtypeStruct((k, arcs), BF16),
            jax.ShapeDtypeStruct((arcs, k), BF16),
            jax.ShapeDtypeStruct((arcs, dem.shape[-1]), F32),
            jax.ShapeDtypeStruct((n, nodes, 256), BF16),
            jax.ShapeDtypeStruct((n, nodes, 256), BF16),
            jax.ShapeDtypeStruct((n, nodes, nodes - 256), BF16),
            jax.ShapeDtypeStruct((n, nodes, nodes - 256), BF16),
    )
    return pl.pallas_call(
        front_kernel,
        out_shape=shapes,
        in_specs=[VM, ANY, VM, VM],
        out_specs=[ANY] * 7,
        scratch_shapes=[pltpu.VMEM(a.shape, a.dtype) for a in shapes] + [
            pltpu.VMEM((n, nodes, arcs), F32),
            pltpu.VMEM((n * nodes // 4, 128), F32),
            pltpu.VMEM((n * nodes // 4, 128), F32),
            pltpu.VMEM((n, nodes, 256), F32),
            pltpu.SemaphoreType.DMA((n,)),
            pltpu.SemaphoreType.DMA((5 + 2 * n,)),
        ],
        compiler_params=pltpu.CompilerParams(vmem_limit_bytes=60 * 2**20),
        name="front",
    )(lf, links, usage, dem.reshape(k, -1))


MESH = pl.DeviceIdType.MESH


def upper_solve(corr, share, dh, dl, lh, ll, out):
    n, nodes, _ = dh.shape
    blocks = nodes // 256
    for k in range(n):
        done = [None] * blocks
        for b in reversed(range(blocks)):
            at = slice(256 * b, 256 * b + 256)
            full = slice(k * nodes + 256 * b, k * nodes + 256 * b + 256)
            rest = share[:, full].astype(F32) - corr[:, full].astype(F32)
            for e in range(b + 1, blocks):
                s = (k, slice(256 * e, 256 * e + 256), at)
                rest = rest - mm3(done[e], (lh[s], ll[s]))
            x = mm3(halves(rest), (dh[k, at, :], dl[k, at, :]))
            done[b] = halves(x)
            out[k, :, at] = x


def middle_kernel(damp, t_in, tt_in, rp_in, dem_in, dh_in, dl_in, lh_in, ll_in, s_out, y_out, st_out, c_out,
                  t, tt, rp, dm, dmt, dh, dl, lh, ll, in_s,
                  near, far, cross, sbuf, r1, mb, m1, r2, m2, r3,
                  a1, a2, a3, b1, b2, ag, rhs16,
                  p0, p1, p2, p3, q1, q2, yg,
                  u_send, u_half, u_got, u_all, c_part, c_send, c_near, c_far,
                  xs, xr, x_s, x_r, tt_s, tt_r, s1x_s, s1x_r, s1z_s, s1z_r, sb_s, sb_r, s2_s, s2_r, s3_s, s3_r,
                  ca_s, ca_r, cb_s, cb_r, cc_s, cc_r, w_s, w_r):
    com, arc = lax.axis_index("com"), lax.axis_index("arc")
    x, z, yh = com // 8, (com // 2) % 4, com % 2
    yl, core = arc // 2, arc % 2
    nearby = yl * 2 + 1 - core
    opposite = (1 - yl) * 2 + core
    diagonal = (1 - yl) * 2 + 1 - core

    def at_x(i):
        return (i * 8 + z * 2 + yh, arc)

    def at_z(i):
        return (x * 8 + i * 2 + yh, arc)

    def other(i, o):
        return (i + o) % 4

    partner = (com, nearby)
    facing = (com, opposite)
    mirror = (x * 8 + z * 2 + 1 - yh, arc)

    loads = [pltpu.make_async_copy(src, dst, in_s.at[i]) for i, (src, dst) in enumerate(
        ((rp_in, rp), (tt_in, tt), (t_in, t), (dem_in, dm), (dh_in, dh), (dl_in, dl), (lh_in, lh), (ll_in, ll)))]
    for c in loads:
        c.start()
    barrier = pltpu.get_barrier_semaphore()
    for peer in [at_x(other(x, o)) for o in (1, 2, 3)] + [at_z(other(z, o)) for o in (1, 2, 3)] + [partner, facing, mirror]:
        pl.semaphore_signal(barrier, inc=1, device_id=peer, device_id_type=MESH)
    split = x // 2 != yl

    @pl.when(split)
    def _():
        for j in range(8):
            pl.semaphore_signal(barrier, inc=1, device_id=(arc * 8 + j, x), device_id_type=MESH)

    pl.semaphore_wait(barrier, jnp.where(split, 17, 9))

    def copy(src, dst, send, recv, peer):
        return pltpu.make_async_remote_copy(src_ref=src, dst_ref=dst, send_sem=send, recv_sem=recv, device_id=peer, device_id_type=MESH)

    firsts, seconds = (x, z), (z, x)
    first_at, second_at = (at_x, at_z), (at_z, at_x)
    pending = []

    def go(c):
        c.start()
        pending.append(c)

    def slab(ref, h, i):
        return ref.at[i, :, :, :, pl.ds(0, 128)] if h == 0 else ref.at[:, i, :, :, pl.ds(128, 128)]

    def rs_first(src, dst, sems, which):
        for h in (0, 1):
            for o in (1, 2, 3):
                p = other(firsts[h], o)
                go(copy(slab(src, h, p), dst.at[h, 3 - o], sems[0].at[which, h, o - 1], sems[1].at[which, h, 3 - o], first_at[h](p)))

    def rs_second(src, one, mine, two, sems, which):
        for h in (0, 1):
            for s in range(3):
                copy(one.at[h, s], one.at[h, s], sems[0].at[which, h, s], sems[1].at[which, h, s], partner).wait_recv()
            own = src[firsts[0], :, :, :, 0:128] if h == 0 else src[:, firsts[1], :, :, 128:256]
            total = own.astype(F32)
            for s in range(3):
                total = total + one[h, s].astype(F32)
            mine[h] = total.astype(mine.dtype)
            for o in (1, 2, 3):
                p = other(seconds[h], o)
                go(copy(mine.at[h, p], two.at[h, 3 - o], sems[2].at[which, h, o - 1], sems[3].at[which, h, 3 - o], second_at[h](p)))

    def rs_third(mine, two, mine2, three, sems, which):
        for h in (0, 1):
            for s in range(3):
                copy(two.at[h, s], two.at[h, s], sems[2].at[which, h, s], sems[3].at[which, h, s], partner).wait_recv()
            total = mine[h, seconds[h]].astype(F32)
            for s in range(3):
                total = total + two[h, s].astype(F32)
            mine2[h] = total.astype(mine2.dtype)
            go(copy(mine2.at[h, 1 - yh], three.at[h], sems[4].at[which, h], sems[5].at[which, h], mirror))

    def rs_done(mine2, three, sems, which, h):
        copy(three.at[h], three.at[h], sems[4].at[which, h], sems[5].at[which, h], mirror).wait_recv()
        return mine2[h, yh].astype(F32) + three[h].astype(F32)

    def ag_first(full, sems, which):
        for h in (0, 1):
            here = full.at[h, firsts[h], seconds[h], yh]
            go(copy(here, here, sems[4].at[which, h], sems[5].at[which, h], mirror))

    def ag_second(full, sems, which):
        for h in (0, 1):
            there = full.at[h, firsts[h], seconds[h], 1 - yh]
            copy(there, there, sems[4].at[which, h], sems[5].at[which, h], mirror).wait_recv()
            here = full.at[h, firsts[h], seconds[h]]
            for o in (1, 2, 3):
                go(copy(here, here, sems[2].at[which, h, o - 1], sems[3].at[which, h, 3 - o], second_at[h](other(seconds[h], o))))

    def ag_third(full, sems, which):
        for h in (0, 1):
            for s in range(3):
                there = full.at[h, firsts[h], other(seconds[h], s + 1)]
                copy(there, there, sems[2].at[which, h, s], sems[3].at[which, h, s], partner).wait_recv()
            here = full.at[h, firsts[h]]
            for o in (1, 2, 3):
                go(copy(here, here, sems[0].at[which, h, o - 1], sems[1].at[which, h, 3 - o], first_at[h](other(firsts[h], o))))

    def ag_done(full, sems, which, out):
        for h in (0, 1):
            for s in range(3):
                there = full.at[h, other(firsts[h], s + 1)]
                copy(there, there, sems[0].at[which, h, s], sems[1].at[which, h, s], partner).wait_recv()
        for i in range(4):
            for j in range(4):
                rows = slice((i * 4 + j) * 64, (i * 4 + j) * 64 + 64)
                out[rows, 0:128] = full[0, i, j].astype(out.dtype).reshape(64, 128)
                out[rows, 128:256] = full[1, j, i].astype(out.dtype).reshape(64, 128)

    sems = (ca_s, ca_r, cb_s, cb_r, cc_s, cc_r)

    def piece(q):
        return pl.ds(pl.multiple_of(q * 32, 32), 32)

    half = t.shape[0] // 2
    given = pl.ds(pl.multiple_of(yl * half, half), half)
    taken = pl.ds(pl.multiple_of((1 - yl) * half, half), half)

    def rows_of(source, block, q):
        whole = source.shape[2] == 2 * half

        @pl.loop(0, 4)
        def _(j):
            cols = pl.ds(pl.multiple_of(j * 256, 256), 256)
            left = source[:, piece(q), :].reshape(256, -1)
            sbuf[block, :, :, piece(q), cols] = mm(left, t[:, cols] if whole else t[taken, cols]).astype(BF16).reshape(4, 2, 32, 256)

    def flip(i):
        return i + 1 - 2 * (i % 2)

    def turn(i):
        return 3 - i

    def ways(q):
        return (flip, turn) if q % 2 == 0 else (turn, flip)

    def x_copy(q, s):
        one, two = ways(q)
        block = one(x) if s == 0 else two(one(x))
        return block, copy(sbuf.at[block, :, :, piece(q), pl.ds(0, 512)], r1.at[0, s, :, :, piece(q)],
                           s1x_s.at[s, q], s1x_r.at[s, q], at_x(one(x)))

    def z_copy(block, q, s):
        one, two = ways(q)
        part = one(z) if s == 0 else two(one(z))
        return copy(sbuf.at[block, part, :, piece(q), pl.ds(512, 512)], r1.at[1, s, block, :, piece(q)],
                    s1z_s.at[s, block, q], s1z_r.at[s, block, q], at_z(one(z)))

    def relay_copy(h, q):
        two = ways(q)[1]
        return copy(mb.at[h, :, :, piece(q)], r1.at[h, 2, :, :, piece(q)], sb_s.at[h, q], sb_r.at[h, q], first_at[h](two(firsts[h])))

    def send_rows(block, q):
        for s in (1, 0):
            z_copy(block, q, s).start()
            wanted, c = x_copy(q, s)
            pl.when(block == wanted)(c.start)

    def fold_zero(q):
        two = ways(q)[1]
        x_copy(q, 1)[1].wait_recv()

        @pl.loop(0, 4)
        def _(i):
            mb[0, i, :, piece(q)] = (sbuf[two(x), i, :, piece(q), 0:512].astype(F32) + r1[0, 1, i, :, piece(q)].astype(F32)).astype(BF16)

        relay_copy(0, q).start()
        for b in range(4):
            z_copy(b, q, 1).wait_recv()

        @pl.loop(0, 4)
        def _(i):
            mb[1, i, :, piece(q)] = (sbuf[i, two(z), :, piece(q), 512:1024].astype(F32) + r1[1, 1, i, :, piece(q)].astype(F32)).astype(BF16)

        relay_copy(1, q).start()

    def fold_first(q):
        x_copy(q, 0)[1].wait_recv()
        for b in range(4):
            z_copy(b, q, 0).wait_recv()
        for h in (0, 1):
            relay_copy(h, q).wait_recv()

            @pl.loop(0, 4)
            def _(i):
                own = sbuf[x, i, :, piece(q), 0:512] if h == 0 else sbuf[i, z, :, piece(q), 512:1024]
                total = own.astype(F32) + r1[h, 0, i, :, piece(q)].astype(F32) + r1[h, 2, i, :, piece(q)].astype(F32)
                m1[h, i, :, piece(q)] = total.astype(BF16)

            for o in (1, 2, 3):
                second_copy(h, q, o).start()

    def second_copy(h, q, o):
        p = other(seconds[h], o)
        return copy(m1.at[h, p, :, piece(q)], r2.at[h, 3 - o, :, piece(q)], s2_s.at[h, q, o - 1], s2_r.at[h, 3 - o, q], second_at[h](p))

    def own_sum(h, q, k):
        if h == 0:
            total = sbuf[x, z, k, piece(q), 0:512].astype(F32)
        else:
            total = sbuf[x, z, k, piece(q), 512:1024].astype(F32)
        for s in (0, 2):
            total = total + r1[h, s, seconds[h], k, piece(q)].astype(F32)
        for s in range(3):
            total = total + r2[h, s, k, piece(q)].astype(F32)
        return total

    def third_copy(h, q):
        return copy(m2.at[h, piece(q)], r3.at[h, piece(q)], s3_s.at[h, q], s3_r.at[h, q], mirror)

    def fold_second(q):
        for h in (0, 1):
            for s in range(3):
                there = r2.at[h, s, :, piece(q)]
                copy(there, there, s2_s.at[h, q, s], s2_r.at[h, s, q], partner).wait_recv()
            m2[h, piece(q)] = own_sum(h, q, 1 - yh).astype(BF16)
            third_copy(h, q).start()

    def fold_third(q):
        for h in (0, 1):
            third_copy(h, q).wait_recv()
            s_out[piece(q), 512 * h:512 * h + 512] = own_sum(h, q, yh) + r3[h, piece(q)].astype(F32)

    loads[0].wait()
    rs_first(rp, a1, sems, 0)
    loads[1].wait()
    go(copy(tt, near, tt_s.at[0], tt_r.at[0], partner))

    def face_copy(q):
        return copy(tt.at[:, piece(q), given], far.at[:, piece(q)], tt_s.at[1 + q], tt_r.at[1 + q], facing)

    def forward_copy(q):
        return copy(far.at[:, piece(q)], cross.at[:, piece(q)], tt_s.at[5 + q], tt_r.at[5 + q], partner)

    def compute_rows(source, block, low, high):
        @pl.loop(low, high)
        def _(q):
            rows_of(source, block, q)

    def far_rows(q):
        face_copy(q).wait_recv()
        go(forward_copy(q))
        rows_of(far, opposite, q)

    def cross_rows(q):
        forward_copy(q).wait_recv()
        rows_of(cross, diagonal, q)

    go(face_copy(0))
    loads[2].wait()
    compute_rows(tt, arc, 0, 4)
    rs_second(rp, a1, b1, a2, sems, 0)
    copy(tt, near, tt_s.at[0], tt_r.at[0], partner).wait_recv()
    compute_rows(near, nearby, 0, 2)
    rs_third(b1, a2, b2, a3, sems, 0)
    send_rows(arc, 0)
    send_rows(nearby, 0)
    compute_rows(near, nearby, 2, 3)
    for h in (0, 1):
        rhs_sum = rs_done(b2, a3, sems, 0, h)
        b2[h, yh] = rhs_sum
        ag[h, firsts[h], seconds[h], yh] = rhs_sum.astype(BF16)
    ag_first(ag, sems, 1)
    compute_rows(near, nearby, 3, 4)
    ag_second(ag, sems, 1)
    go(face_copy(1))
    ag_third(ag, sems, 1)
    ag_done(ag, sems, 1, rhs16)
    send_rows(arc, 1)
    send_rows(nearby, 1)
    send_rows(arc, 2)
    send_rows(nearby, 2)

    mine_rows = pl.ds(pl.multiple_of(core * half, half), half)
    other_rows = pl.ds(pl.multiple_of((1 - core) * half, half), half)
    u_send[0] = mm(t[other_rows, :], rhs16[...]).astype(BF16)
    go(copy(u_send.at[0], u_got.at[0], w_s.at[0], w_r.at[0], partner))
    u_half[...] = mm(t[mine_rows, :], rhs16[...])
    copy(u_got.at[0], u_got.at[0], w_s.at[0], w_r.at[0], partner).wait_recv()
    u_half[...] += u_got[0].astype(F32)
    u_send[1] = u_half[...].astype(BF16)
    go(copy(u_send.at[1], u_got.at[1], w_s.at[1], w_r.at[1], facing))
    go(face_copy(2))
    far_rows(0)
    cross_rows(0)
    send_rows(arc, 3)
    send_rows(nearby, 3)
    copy(u_got.at[1], u_got.at[1], w_s.at[1], w_r.at[1], facing).wait_recv()
    u_all[core] = (u_half[...] + u_got[1].astype(F32)).astype(BF16)
    go(copy(u_all.at[core], u_all.at[core], w_s.at[2], w_r.at[2], partner))
    far_rows(1)
    there = u_all.at[1 - core]
    copy(there, there, w_s.at[2], w_r.at[2], partner).wait_recv()

    @pl.loop(0, 8)
    def _(j):
        left = tt[j]
        part = mm(left[:, 0:half], u_all[0]) + mm(left[:, half:], u_all[1])
        p0[j // 2, pl.ds(2 * (j % 2), 2)] = part.astype(BF16).reshape(2, 2, 32, 256)

    rs_first(p0, p1, sems, 2)
    cross_rows(1)
    rs_second(p0, p1, q1, p2, sems, 2)
    rs_third(q1, p2, q2, p3, sems, 2)
    send_rows(opposite, 0)
    send_rows(diagonal, 0)
    lanes = lax.broadcasted_iota(jnp.int32, (32, 128), 1)
    place = lax.broadcasted_iota(jnp.int32, (32, 128), 0) + (com % 4) * 32
    scale = jnp.sum(jnp.where(lanes == place, damp[pl.ds(com // 4, 1), :], 0.0), axis=1, keepdims=True)
    for h in (0, 1):
        prod = rs_done(q2, p3, sems, 2, h)
        yg[h, firsts[h], seconds[h], yh] = (b2[h, yh] - scale * prod).astype(BF16)
    ag_first(yg, sems, 3)
    send_rows(opposite, 1)
    ag_second(yg, sems, 3)
    go(face_copy(3))
    fold_zero(0)
    far_rows(2)
    ag_third(yg, sems, 3)
    send_rows(diagonal, 1)
    cross_rows(2)
    fold_first(0)
    ag_done(yg, sems, 3, y_out)
    send_rows(opposite, 2)
    send_rows(diagonal, 2)

    @pl.loop(0, 4)
    def _(j):
        rows = pl.ds(pl.multiple_of(j * 256, 256), 256)
        left = y_out[rows, :].astype(F32).T.astype(BF16)
        right = tt[pl.ds(2 * j, 2)].reshape(256, -1)
        part = mm(left, right)

        @pl.when(j == 0)
        def _():
            c_part[...] = part.reshape(c_part.shape)

        @pl.when(j > 0)
        def _():
            c_part[...] += part.reshape(c_part.shape)

    c_send[0:2] = c_part[:, 1 - core].astype(BF16)
    go(copy(c_send.at[pl.ds(0, 2)], c_near, w_s.at[3], w_r.at[3], partner))
    fold_zero(1)
    far_rows(3)
    send_rows(opposite, 3)
    copy(c_near, c_near, w_s.at[3], w_r.at[3], partner).wait_recv()
    c_send[2] = (c_part[1 - yl, core] + c_near[1 - yl].astype(F32)).astype(BF16)
    go(copy(c_send.at[2], c_far, w_s.at[4], w_r.at[4], facing))
    cross_rows(3)
    send_rows(diagonal, 3)
    fold_first(1)
    fold_zero(2)
    fold_second(0)
    fold_zero(3)
    fold_second(1)
    fold_first(2)
    fold_third(0)
    fold_first(3)
    fold_third(1)
    copy(c_far, c_far, w_s.at[4], w_r.at[4], facing).wait_recv()
    c_out[...] = c_part[yl, core] + c_near[yl].astype(F32) + c_far[...].astype(F32)
    for c in loads[3:]:
        c.wait()
    for b in range(6):
        dmt[:, 256 * b:256 * b + 256] = dm[256 * b:256 * b + 256, :].astype(F32).T
    upper_solve(c_out, dmt.at[pl.ds(pl.multiple_of(arc * 64, 64), 64)], dh, dl, lh, ll, st_out)
    fold_second(2)
    fold_second(3)
    fold_third(2)
    fold_third(3)

    def swap_copy(j, slot):
        return copy(xs.at[j], xr.at[slot], x_s.at[j], x_r.at[slot], (arc * 8 + j, x))

    @pl.when(split)
    def _():
        for j in range(8):
            xs[j] = s_out[:, 128 * j:128 * j + 128].astype(BF16)
        for j in range(8):
            swap_copy(j, z * 2 + yh).start()
        for j in range(8):
            swap_copy(j, j).wait_recv()
            s_out[:, 128 * j:128 * j + 128] += xr[j].astype(F32).T
        for j in range(8):
            swap_copy(j, z * 2 + yh).wait_send()

    for c in pending:
        c.wait_send()

    for q in range(4):
        for s in (0, 1):
            for block in range(4):
                z_copy(block, q, s).wait_send()
            x_copy(q, s)[1].wait_send()
        for h in (0, 1):
            relay_copy(h, q).wait_send()
        for h in (0, 1):
            for o in (1, 2, 3):
                second_copy(h, q, o).wait_send()
            third_copy(h, q).wait_send()


def middle(t, tt, rhs_part, damping, dem, dh, dl, lh, ll):
    rows, arcs = t.shape
    scen = rhs_part.shape[1]
    V, DMA = pltpu.VMEM, pltpu.SemaphoreType.DMA
    tt = tt.reshape(8, 128, rows)
    return pl.pallas_call(
        middle_kernel,
        out_shape=(
            jax.ShapeDtypeStruct((128, arcs), F32),
            jax.ShapeDtypeStruct((arcs, scen), BF16),
            jax.ShapeDtypeStruct((dh.shape[0], 64, dh.shape[1]), F32),
        ),
        in_specs=[VM] + [ANY] * 8,
        out_specs=[VM] * 3,
        scratch_shapes=[
            V((64, rows), F32), V((rows, arcs), BF16), V((8, 128, rows), BF16), V((4, 4, 2, 32, scen), F32),
            V((rows, scen), BF16), V((scen, rows), F32), V(dh.shape, BF16), V(dl.shape, BF16), V(lh.shape, BF16), V(ll.shape, BF16), DMA((8,)),
            V((8, 128, rows), BF16), V((8, 128, rows // 2), BF16), V((8, 128, rows // 2), BF16),
            V((4, 4, 2, 128, arcs), BF16),
            V((2, 3, 4, 2, 128, 512), BF16), V((2, 4, 2, 128, 512), BF16), V((2, 4, 2, 128, 512), BF16),
            V((2, 3, 2, 128, 512), BF16), V((2, 128, 512), BF16), V((2, 128, 512), BF16),
            V((2, 3, 4, 2, 32, 128), F32), V((2, 3, 2, 32, 128), F32), V((2, 32, 128), F32),
            V((2, 4, 2, 32, 128), F32), V((2, 2, 32, 128), F32),
            V((2, 4, 4, 2, 32, 128), BF16), V((arcs, scen), BF16),
            V((4, 4, 2, 32, 256), BF16),
            V((2, 3, 4, 2, 32, 128), BF16), V((2, 3, 2, 32, 128), BF16), V((2, 32, 128), BF16),
            V((2, 4, 2, 32, 128), BF16), V((2, 2, 32, 128), BF16),
            V((2, 4, 4, 2, 32, 128), BF16),
            V((2, rows // 2, scen), BF16), V((rows // 2, scen), F32), V((2, rows // 2, scen), BF16),
            V((2, rows // 2, scen), BF16),
            V((2, 2, 64, rows), F32), V((3, 64, rows), BF16), V((2, 64, rows), BF16), V((64, rows), BF16),
            V((8, 128, 128), BF16), V((8, 128, 128), BF16), DMA((8,)), DMA((8,)),
            DMA((9,)), DMA((9,)),
            DMA((2, 4)), DMA((2, 4)), DMA((2, 4, 4)), DMA((2, 4, 4)), DMA((2, 4)), DMA((2, 4)),
            DMA((2, 4, 3)), DMA((2, 3, 4)), DMA((2, 4)), DMA((2, 4)),
            DMA((4, 2, 3)), DMA((4, 2, 3)), DMA((4, 2, 3)), DMA((4, 2, 3)), DMA((4, 2)), DMA((4, 2)),
            DMA((5,)), DMA((5,)),
        ],
        compiler_params=pltpu.CompilerParams(
            vmem_limit_bytes=63 * 2**20, collective_id=0, has_side_effects=True
        ),
        name="middle",
    )(damping.reshape(8, 128), t, tt, rhs_part.reshape(4, 4, 2, 32, scen), dem, dh, dl, lh, ll)


def write_kernel(schur, y, steps, schur_out, y_out, steps_out):
    schur_out[...] = schur[...]
    y_out[...] = y[...].astype(F32)
    steps_out[...] = steps[...]


def write(*arrays):
    return pl.pallas_call(
        write_kernel,
        out_shape=tuple(jax.ShapeDtypeStruct(a.shape, F32) for a in arrays),
        in_specs=[VM] * 3,
        out_specs=[VM] * 3,
        name="write",
    )(*arrays)


def on_device(lfactor, links, usage, demands, damping):
    n, nodes, arcs = links.shape
    dem = demands.reshape(n * nodes, demands.shape[2])
    t, tt, rhs_part, dh, dl, lh, ll = front(lfactor, links, usage, dem)
    schur, y, steps = write(*middle(t, tt, rhs_part, damping, dem, dh, dl, lh, ll))
    return schur, y, steps.transpose(0, 2, 1)


def solution(mesh):
    return jax.shard_map(
        on_device,
        mesh=mesh,
        in_specs=(P("com"), P("com", None, "arc"), P("com", "arc"), P("com"), P("arc")),
        out_specs=(P("com", "arc"), P("arc"), P("com", None, "arc")),
        check_vma=False,
    )
```
